256 devices in a mesh: lon: 16 (over y_hi, z), lat: 8 (over x, core), band: 2 (over y_lo).
Axes of the slice: x: 4, y: 4 (y_hi: 2, y_lo: 2; y = y_hi * 2 + y_lo), z: 8, core: 2. Of those that a mesh axis runs over, the one named last changes fastest.
Arguments:
- spectrum: float32 [128, 256, 576], P('lat', 'lon', 'band'), may hold values from 0.02 to 13, as said below
- sea_mask: int32 [128, 256], P('lat', 'lon'), may hold values 0 or 1
- ice_mask: int32 [128, 256], P('lat', 'lon'), may hold values 0 or 1
- depth_class: int32 [128, 256], P('lat', 'lon'), may hold values from 0 to 7
- speed_table: float32 [8, 16], replicated, may hold values from 0.2 to 0.8
- refraction_table: float32 [8, 16], replicated, may hold values from 0.05 to 0.5
- depth_slope: float32 [2, 128, 256], P(None, 'lat', 'lon'), may hold values from -1 to 1
- wind_speed: float32 [128, 256], P('lat', 'lon'), may hold values from 0.3 to 3
- wind_dir: float32 [128, 256], P('lat', 'lon'), may hold values from -3.140625 to 3.140625
- ice_rate: float32 [16], replicated, may hold values from 0.1 to 1
Outputs:
- spectrum_out: float32 [128, 256, 576], P('lat', 'lon', 'band')
The draws below stay inside these ranges and needn't reach their ends.
Inputs may be any that keep to these rules, and one draw needn't show every extreme that they name: `spectrum`: densities are positive.
All inputs are finite; a program needn't handle non-finite values. No bound on the sum of `sea_mask` or of `ice_mask` on one device may be relied on, other than what follows from the above.
Results may differ from the reference program's by a relative error of at most 0.0003.
Values sent between devices are 32-bit elements; how exact they have to be, the bound alone decides.
A program may use at most 64 MiB of HBM per device.

```python
import math
import jax
import jax.numpy as jnp
from jax import lax

NFREQ = 16
NDIR = 36
NCLASS = 8
ITERS = 4
NCOMP = 576
NLAT = 128
NLON = 256


def draw_spectrum(key, part):
    base_key, comp_key, point_key = jax.random.split(key, 3)
    noise_draw = jax.random.uniform(base_key, (NLAT, NLON, NCOMP), jnp.float32)
    comp_draw = jax.random.uniform(comp_key, (1, 1, NCOMP), jnp.float32)
    point_draw = jax.random.uniform(point_key, (NLAT, NLON, 1), jnp.float32)
    base_value = jnp.exp(math.log(0.3) + noise_draw * math.log(10.0))
    comp_scale = jnp.exp((comp_draw - 0.5) * math.log(4.0))
    point_scale = jnp.exp((point_draw - 0.5) * math.log(3.0))
    return base_value * comp_scale * point_scale


def with_ends(values, own_key, low, high):
    index_at = [jax.random.randint(jax.random.fold_in(own_key, axis), (), 0, length) for axis, length in enumerate(values.shape)]
    main_axis = values.shape.index(max(values.shape))
    next_to = index_at[:main_axis] + [(index_at[main_axis] + 1) % values.shape[main_axis]] + index_at[main_axis + 1:]
    return values.at[tuple(index_at)].set(low).at[tuple(next_to)].set(high)


def steps_of(key, shape, pieces, least, largest):
    def one(dim, blocks):
        steps = jax.random.uniform(jax.random.fold_in(jax.random.fold_in(key, 6), dim), (blocks,), jnp.float32, least / len(pieces), largest / len(pieces))
        return jnp.repeat(jnp.exp(steps), shape[dim] // blocks).reshape((-1,) + (1,) * (len(shape) - dim - 1))

    gain = one(*pieces[0])
    for cut in pieces[1:]:
        gain = gain * one(*cut)
    return gain


def setup_inputs(seed: int = 0) -> dict:
    splits = jax.random.split(jax.random.key(seed), 11)
    spectrum = draw_spectrum(jax.random.fold_in(splits[10], 71), 0)
    sea_mask = with_ends((jax.random.randint(splits[1], (NLAT, NLON), 0, 10) < 9).astype(jnp.int32), jax.random.fold_in(splits[1], 1), 0, 1)
    ice_mask = with_ends((jax.random.randint(splits[2], (NLAT, NLON), 0, 5) < 1).astype(jnp.int32), jax.random.fold_in(splits[2], 1), 0, 1)
    depth_class = with_ends(jax.random.randint(splits[3], (NLAT, NLON), 0, NCLASS), jax.random.fold_in(splits[3], 1), 0, NCLASS - 1).astype(jnp.int32)
    speed_table = jnp.clip(jax.random.uniform(splits[4], (NCLASS, NFREQ), jnp.float32, 0.2, 0.8), 0.2, 0.8)
    refraction_table = jnp.clip(jax.random.uniform(splits[5], (NCLASS, NFREQ), jnp.float32, 0.05, 0.5), 0.05, 0.5)
    depth_slope = jnp.clip(jax.random.uniform(splits[6], (2, NLAT, NLON), jnp.float32, -1.0, 1.0) * steps_of(splits[6], (2, NLAT, NLON), ((1, 8), (2, 16)), -0.4, 0.0), -1.0, 1.0)
    wind_speed = jnp.clip(jnp.exp(math.log(3.0) - 2.3025851 * jax.random.uniform(splits[7], (NLAT, NLON), jnp.float32) ** steps_of(splits[7], (NLAT, NLON), ((0, 8), (1, 16)), -0.2, 0.2)), 0.3, 3.0)
    wind_dir = jnp.clip(jax.random.uniform(splits[8], (NLAT, NLON), jnp.float32, -3.140625, 3.140625), -3.140625, 3.140625)
    ice_rate = jnp.clip(jnp.exp(jax.random.uniform(splits[9], (NFREQ,), jnp.float32, math.log(0.1), math.log(1.0))), 0.1, 1.0)
    return dict(spectrum=spectrum, sea_mask=sea_mask, ice_mask=ice_mask, depth_class=depth_class, speed_table=speed_table, refraction_table=refraction_table, depth_slope=depth_slope, wind_speed=wind_speed, wind_dir=wind_dir, ice_rate=ice_rate)


freq_ratio = 1.1
wind_gain = 0.12
break_coef = 0.05
south_edge = -30.0
band_span = 60.0


def quickest(behind, center, forward, beyond, courant):
    curvature = jnp.where(courant >= 0.0, forward - 2.0 * center + behind, beyond - 2.0 * forward + center)
    face_value = 0.5 * (center + forward) - 0.5 * courant * (forward - center) - (1.0 - courant * courant) / 6.0 * curvature
    return courant * face_value


def advect(density, cell_speed, axis_dim):
    length = density.shape[axis_dim]

    def piece(array, low, high):
        return lax.slice_in_dim(array, low, high, axis=axis_dim)

    courant = 0.5 * (piece(cell_speed, 1, length - 2) + piece(cell_speed, 2, length - 1))
    fluxes = quickest(piece(density, 0, length - 3), piece(density, 1, length - 2), piece(density, 2, length - 1), piece(density, 3, length), courant)
    faces = fluxes.shape[axis_dim]
    return piece(density, 2, length - 2) - (piece(fluxes, 1, faces) - piece(fluxes, 0, faces - 1))


def rotate(density, offset):
    dir_index = jnp.arange(density.shape[-1]) % NDIR
    target = dir_index + offset
    inner_roll = jnp.roll(density, -offset, axis=-1)
    if offset > 0:
        outer_roll = jnp.roll(density, NDIR - offset, axis=-1)
        return jnp.where(target >= NDIR, outer_roll, inner_roll)
    outer_roll = jnp.roll(density, -(offset + NDIR), axis=-1)
    return jnp.where(target < 0, outer_roll, inner_roll)


def refract(density, courant):
    fluxes = quickest(rotate(density, -1), density, rotate(density, 1), rotate(density, 2), courant)
    return density - (fluxes - rotate(fluxes, -1))


def expand(per_freq, spread):
    return jnp.dot(per_freq, spread, precision=lax.Precision.HIGHEST)


def lookup(classes, lookup_table):
    onehot = (classes[..., None] == jnp.arange(lookup_table.shape[0])).astype(jnp.float32)
    return jnp.dot(onehot, lookup_table, precision=lax.Precision.HIGHEST)


def stretch(rows, total_rows):
    latitude = (south_edge + band_span * (rows.astype(jnp.float32) + 0.5) / total_rows) * (math.pi / 180.0)
    return 1.0 / jnp.cos(latitude)


def sources(density, energy_sum, moment, levels, heading, ice_loss, sea_share, ice_share, wind_speed, wind_dir):
    mean_level = jnp.maximum(moment, 1.0) / jnp.maximum(energy_sum, 1.0)
    energy = energy_sum / NCOMP
    breaking = break_coef * levels * levels / mean_level[..., None] * (energy * energy)[..., None]
    growth = wind_gain * wind_speed[..., None] * levels * jnp.maximum(jnp.cos(heading - wind_dir[..., None]), 0.0)
    damping = ice_share[..., None] * ice_loss
    return sea_share[..., None] * density * jnp.exp(growth - breaking - damping)


def wrap_cols(array):
    return jnp.concatenate([array[:, -2:], array, array[:, :2]], axis=1)


def pad_rows(array):
    return jnp.pad(array, ((2, 2), (0, 0), (0, 0)))


def reference(spectrum, sea_mask, ice_mask, depth_class, speed_table, refraction_table, depth_slope, wind_speed, wind_dir, ice_rate):
    sea_share = sea_mask.astype(jnp.float32)
    ice_share = ice_mask.astype(jnp.float32)
    comp_index = jnp.arange(NCOMP)
    spread = (comp_index[None, :] // NDIR == jnp.arange(NFREQ)[:, None]).astype(jnp.float32)
    heading = 2.0 * math.pi * (comp_index % NDIR).astype(jnp.float32) / NDIR
    levels = jnp.exp(math.log(freq_ratio) * (comp_index // NDIR).astype(jnp.float32))
    ice_loss = jnp.repeat(ice_rate, NDIR)
    group_speed = lookup(depth_class, speed_table) * sea_share[..., None]
    turning = lookup(depth_class, refraction_table) * sea_share[..., None]
    stretch_rows = stretch(jnp.arange(NLAT), NLAT)
    cell_speed = expand(group_speed, spread)
    along_x = cell_speed * jnp.cos(heading) * stretch_rows[:, None, None]
    along_y = cell_speed * jnp.sin(heading)
    face_angle = heading + math.pi / NDIR
    along_t = expand(turning * depth_slope[0][..., None], spread) * jnp.sin(face_angle) - expand(turning * depth_slope[1][..., None], spread) * jnp.cos(face_angle)
    density = spectrum * sea_share[..., None]
    for substep in range(ITERS):
        density = advect(wrap_cols(density), wrap_cols(along_x), 1)
        density = advect(pad_rows(density), pad_rows(along_y), 0)
        density = refract(density, along_t)
    energy_sum = jnp.sum(density, axis=-1)
    moment = jnp.sum(density * levels, axis=-1)
    return sources(density, energy_sum, moment, levels, heading, ice_loss, sea_share, ice_share, wind_speed, wind_dir)
```

```python
import math

import jax
import jax.numpy as jnp
from jax import lax
from jax.sharding import PartitionSpec as P

NDIR = 36
ITERS = 4
NCOMP = 576


freq_ratio = 1.1
wind_gain = 0.12
break_coef = 0.05
south_edge = -30.0
band_span = 60.0


def quickest(behind, center, forward, beyond, courant):
    curvature = jnp.where(
        courant >= 0.0, forward - 2.0 * center + behind, beyond - 2.0 * forward + center
    )
    face_value = (
        0.5 * (center + forward)
        - 0.5 * courant * (forward - center)
        - (1.0 - courant * courant) / 6.0 * curvature
    )
    return courant * face_value


def advect(density, cell_speed, axis_dim):
    length = density.shape[axis_dim]

    def piece(array, low, high):
        return lax.slice_in_dim(array, low, high, axis=axis_dim)

    courant = 0.5 * (piece(cell_speed, 1, length - 2) + piece(cell_speed, 2, length - 1))
    fluxes = quickest(
        piece(density, 0, length - 3),
        piece(density, 1, length - 2),
        piece(density, 2, length - 1),
        piece(density, 3, length),
        courant,
    )
    faces = fluxes.shape[axis_dim]
    return piece(density, 2, length - 2) - (piece(fluxes, 1, faces) - piece(fluxes, 0, faces - 1))


def rotate(density, offset):
    dir_index = jnp.arange(density.shape[-1]) % NDIR
    target = dir_index + offset
    inner_roll = jnp.roll(density, -offset, axis=-1)
    if offset > 0:
        outer_roll = jnp.roll(density, NDIR - offset, axis=-1)
        return jnp.where(target >= NDIR, outer_roll, inner_roll)
    outer_roll = jnp.roll(density, -(offset + NDIR), axis=-1)
    return jnp.where(target < 0, outer_roll, inner_roll)


def refract(density, courant):
    fluxes = quickest(rotate(density, -1), density, rotate(density, 1), rotate(density, 2), courant)
    return density - (fluxes - rotate(fluxes, -1))


def expand(per_freq, spread):
    return jnp.dot(per_freq, spread, precision=lax.Precision.HIGHEST)


def lookup(classes, lookup_table):
    onehot = (classes[..., None] == jnp.arange(lookup_table.shape[0])).astype(jnp.float32)
    return jnp.dot(onehot, lookup_table, precision=lax.Precision.HIGHEST)


def stretch(rows, total_rows):
    latitude = (south_edge + band_span * (rows.astype(jnp.float32) + 0.5) / total_rows) * (
        math.pi / 180.0
    )
    return 1.0 / jnp.cos(latitude)


def sources(
    density,
    energy_sum,
    moment,
    levels,
    heading,
    ice_loss,
    sea_share,
    ice_share,
    wind_speed,
    wind_dir,
):
    mean_level = jnp.maximum(moment, 1.0) / jnp.maximum(energy_sum, 1.0)
    energy = energy_sum / NCOMP
    breaking = break_coef * levels * levels / mean_level[..., None] * (energy * energy)[..., None]
    growth = (
        wind_gain
        * wind_speed[..., None]
        * levels
        * jnp.maximum(jnp.cos(heading - wind_dir[..., None]), 0.0)
    )
    damping = ice_share[..., None] * ice_loss
    return sea_share[..., None] * density * jnp.exp(growth - breaking - damping)


def exchange(cells, axis, dim, width, closed):
    count = lax.axis_size(axis)
    ends = count if closed else count - 1
    head = lax.slice_in_dim(cells, 0, width, axis=dim)
    tail = lax.slice_in_dim(cells, cells.shape[dim] - width, cells.shape[dim], axis=dim)
    before = lax.ppermute(tail, axis, [(i, (i + 1) % count) for i in range(ends)])
    after = lax.ppermute(head, axis, [((i + 1) % count, i) for i in range(ends)])
    return jnp.concatenate([before, cells, after], axis=dim)


def trim(array, dim, amount):
    return lax.slice_in_dim(array, amount, array.shape[dim] - amount, axis=dim)


def per_device(
    spectrum,
    sea_mask,
    ice_mask,
    depth_class,
    speed_table,
    refraction_table,
    depth_slope,
    wind_speed,
    wind_dir,
    ice_rate,
):
    rows_dev, cols_dev, comps_dev = spectrum.shape
    freqs_dev = comps_dev // NDIR
    halo = 2 * ITERS
    band_index = lax.axis_index("band")
    first_comp = band_index * comps_dev
    local_comp = jnp.arange(comps_dev)
    comp_index = first_comp + local_comp
    spread = (local_comp[None, :] // NDIR == jnp.arange(freqs_dev)[:, None]).astype(jnp.float32)
    heading = 2.0 * math.pi * (comp_index % NDIR).astype(jnp.float32) / NDIR
    face_angle = heading + math.pi / NDIR
    cos_head = jnp.cos(heading)
    sin_head = jnp.sin(heading)
    sin_face = jnp.sin(face_angle)
    cos_face = jnp.cos(face_angle)
    sea_share = sea_mask.astype(jnp.float32)
    ice_share = ice_mask.astype(jnp.float32)
    speed_local = lax.dynamic_slice_in_dim(speed_table, band_index * freqs_dev, freqs_dev, 1)
    refr_local = lax.dynamic_slice_in_dim(refraction_table, band_index * freqs_dev, freqs_dev, 1)
    group_speed = lookup(depth_class, speed_local) * sea_share[..., None]
    turning = lookup(depth_class, refr_local) * sea_share[..., None]
    turn_x = turning * depth_slope[0][..., None]
    turn_y = turning * depth_slope[1][..., None]
    density = spectrum * sea_share[..., None]

    fields = jnp.concatenate([group_speed, turn_x, turn_y], axis=-1)
    density, fields = [exchange(a, "lon", 1, halo, True) for a in (density, fields)]
    density, fields = [exchange(a, "lat", 0, halo, False) for a in (density, fields)]

    total_rows = rows_dev * lax.axis_size("lat")
    first_row = lax.axis_index("lat") * rows_dev - halo
    rows_ext = first_row + jnp.arange(rows_dev + 2 * halo)
    inside = ((rows_ext >= 0) & (rows_ext < total_rows))[:, None, None]
    stretch_rows = stretch(rows_ext, total_rows)
    gs_ext = expand(fields[..., :freqs_dev], spread)
    along_x = gs_ext * cos_head * stretch_rows[:, None, None]
    along_y = gs_ext * sin_head
    along_t = (
        expand(fields[..., freqs_dev : 2 * freqs_dev], spread) * sin_face
        - expand(fields[..., 2 * freqs_dev :], spread) * cos_face
    )
    for substep in range(ITERS):
        density = advect(density, along_x, 1)
        along_x, along_y, along_t = [trim(a, 1, 2) for a in (along_x, along_y, along_t)]
        density = advect(density, along_y, 0)
        inside = trim(inside, 0, 2)
        density = jnp.where(inside, density, 0.0)
        along_x, along_y, along_t = [trim(a, 0, 2) for a in (along_x, along_y, along_t)]
        density = refract(density, along_t)

    levels = jnp.exp(math.log(freq_ratio) * (comp_index // NDIR).astype(jnp.float32))
    ice_loss = lax.dynamic_slice_in_dim(jnp.repeat(ice_rate, NDIR), first_comp, comps_dev, 0)
    partial = jnp.stack([jnp.sum(density, axis=-1), jnp.sum(density * levels, axis=-1)])
    other = lax.ppermute(partial, "band", [(0, 1), (1, 0)])
    energy_sum = partial[0] + other[0]
    moment = partial[1] + other[1]
    return sources(
        density,
        energy_sum,
        moment,
        levels,
        heading,
        ice_loss,
        sea_share,
        ice_share,
        wind_speed,
        wind_dir,
    )


def solution(mesh):
    return jax.shard_map(
        per_device,
        mesh=mesh,
        in_specs=(
            P("lat", "lon", "band"),
            P("lat", "lon"),
            P("lat", "lon"),
            P("lat", "lon"),
            P(),
            P(),
            P(None, "lat", "lon"),
            P("lat", "lon"),
            P("lat", "lon"),
            P(),
        ),
        out_specs=P("lat", "lon", "band"),
        check_vma=False,
    )
```

```python
import math

import jax
import jax.numpy as jnp
from jax import lax
from jax.sharding import PartitionSpec as P

NDIR = 36
ITERS = 4
NCOMP = 576


freq_ratio = 1.1
wind_gain = 0.12
break_coef = 0.05
south_edge = -30.0
band_span = 60.0


def quickest(behind, center, forward, beyond, courant):
    curvature = jnp.where(
        courant >= 0.0, forward - 2.0 * center + behind, beyond - 2.0 * forward + center
    )
    face_value = (
        0.5 * (center + forward)
        - 0.5 * courant * (forward - center)
        - (1.0 - courant * courant) / 6.0 * curvature
    )
    return courant * face_value


def advect(density, cell_speed, axis_dim):
    length = density.shape[axis_dim]

    def piece(array, low, high):
        return lax.slice_in_dim(array, low, high, axis=axis_dim)

    courant = 0.5 * (piece(cell_speed, 1, length - 2) + piece(cell_speed, 2, length - 1))
    fluxes = quickest(
        piece(density, 0, length - 3),
        piece(density, 1, length - 2),
        piece(density, 2, length - 1),
        piece(density, 3, length),
        courant,
    )
    faces = fluxes.shape[axis_dim]
    return piece(density, 2, length - 2) - (piece(fluxes, 1, faces) - piece(fluxes, 0, faces - 1))


def rotate(density, offset):
    dir_index = jnp.arange(density.shape[-1]) % NDIR
    target = dir_index + offset
    inner_roll = jnp.roll(density, -offset, axis=-1)
    if offset > 0:
        outer_roll = jnp.roll(density, NDIR - offset, axis=-1)
        return jnp.where(target >= NDIR, outer_roll, inner_roll)
    outer_roll = jnp.roll(density, -(offset + NDIR), axis=-1)
    return jnp.where(target < 0, outer_roll, inner_roll)


def refract(density, courant):
    fluxes = quickest(rotate(density, -1), density, rotate(density, 1), rotate(density, 2), courant)
    return density - (fluxes - rotate(fluxes, -1))


def expand(per_freq, spread):
    return jnp.dot(per_freq, spread, precision=lax.Precision.HIGHEST)


def lookup(classes, lookup_table):
    onehot = (classes[..., None] == jnp.arange(lookup_table.shape[0])).astype(jnp.float32)
    return jnp.dot(onehot, lookup_table, precision=lax.Precision.HIGHEST)


def stretch(rows, total_rows):
    latitude = (south_edge + band_span * (rows.astype(jnp.float32) + 0.5) / total_rows) * (
        math.pi / 180.0
    )
    return 1.0 / jnp.cos(latitude)


def sources(
    density,
    energy_sum,
    moment,
    levels,
    heading,
    ice_loss,
    sea_share,
    ice_share,
    wind_speed,
    wind_dir,
):
    mean_level = jnp.maximum(moment, 1.0) / jnp.maximum(energy_sum, 1.0)
    energy = energy_sum / NCOMP
    breaking = break_coef * levels * levels / mean_level[..., None] * (energy * energy)[..., None]
    growth = (
        wind_gain
        * wind_speed[..., None]
        * levels
        * jnp.maximum(jnp.cos(heading - wind_dir[..., None]), 0.0)
    )
    damping = ice_share[..., None] * ice_loss
    return sea_share[..., None] * density * jnp.exp(growth - breaking - damping)


def exchange(cells, axis, dim, width, closed):
    count = lax.axis_size(axis)
    ends = count if closed else count - 1
    head = lax.slice_in_dim(cells, 0, width, axis=dim)
    tail = lax.slice_in_dim(cells, cells.shape[dim] - width, cells.shape[dim], axis=dim)
    before = lax.ppermute(tail, axis, [(i, (i + 1) % count) for i in range(ends)])
    after = lax.ppermute(head, axis, [((i + 1) % count, i) for i in range(ends)])
    return jnp.concatenate([before, cells, after], axis=dim)


def trim(array, dim, amount):
    return lax.slice_in_dim(array, amount, array.shape[dim] - amount, axis=dim)


def per_device(
    spectrum,
    sea_mask,
    ice_mask,
    depth_class,
    speed_table,
    refraction_table,
    depth_slope,
    wind_speed,
    wind_dir,
    ice_rate,
):
    rows_dev, cols_dev, comps_dev = spectrum.shape
    freqs_dev = comps_dev // NDIR
    halo = 2 * ITERS
    band_index = lax.axis_index("band")
    first_comp = band_index * comps_dev
    local_comp = jnp.arange(comps_dev)
    comp_index = first_comp + local_comp
    spread = (local_comp[None, :] // NDIR == jnp.arange(freqs_dev)[:, None]).astype(jnp.float32)
    heading = 2.0 * math.pi * (comp_index % NDIR).astype(jnp.float32) / NDIR
    face_angle = heading + math.pi / NDIR
    cos_head = jnp.cos(heading)
    sin_head = jnp.sin(heading)
    sin_face = jnp.sin(face_angle)
    cos_face = jnp.cos(face_angle)
    sea_share = sea_mask.astype(jnp.float32)
    ice_share = ice_mask.astype(jnp.float32)
    speed_local = lax.dynamic_slice_in_dim(speed_table, band_index * freqs_dev, freqs_dev, 1)
    refr_local = lax.dynamic_slice_in_dim(refraction_table, band_index * freqs_dev, freqs_dev, 1)
    group_speed = lookup(depth_class, speed_local) * sea_share[..., None]
    turning = lookup(depth_class, refr_local) * sea_share[..., None]
    turn_x = turning * depth_slope[0][..., None]
    turn_y = turning * depth_slope[1][..., None]
    density = spectrum * sea_share[..., None]

    stacked = jnp.concatenate([density, group_speed, turn_x, turn_y], axis=-1)
    stacked = exchange(exchange(stacked, "lon", 1, halo, True), "lat", 0, halo, False)
    density = stacked[..., :comps_dev]
    fields = stacked[..., comps_dev:]

    total_rows = rows_dev * lax.axis_size("lat")
    first_row = lax.axis_index("lat") * rows_dev - halo
    rows_ext = first_row + jnp.arange(rows_dev + 2 * halo)
    inside = ((rows_ext >= 0) & (rows_ext < total_rows))[:, None, None]
    stretch_rows = stretch(rows_ext, total_rows)
    gs_ext = expand(fields[..., :freqs_dev], spread)
    along_x = gs_ext * cos_head * stretch_rows[:, None, None]
    along_y = gs_ext * sin_head
    along_t = (
        expand(fields[..., freqs_dev : 2 * freqs_dev], spread) * sin_face
        - expand(fields[..., 2 * freqs_dev :], spread) * cos_face
    )
    for substep in range(ITERS):
        density = advect(density, along_x, 1)
        along_x, along_y, along_t = [trim(a, 1, 2) for a in (along_x, along_y, along_t)]
        density = advect(density, along_y, 0)
        inside = trim(inside, 0, 2)
        density = jnp.where(inside, density, 0.0)
        along_x, along_y, along_t = [trim(a, 0, 2) for a in (along_x, along_y, along_t)]
        density = refract(density, along_t)

    levels = jnp.exp(math.log(freq_ratio) * (comp_index // NDIR).astype(jnp.float32))
    ice_loss = lax.dynamic_slice_in_dim(jnp.repeat(ice_rate, NDIR), first_comp, comps_dev, 0)
    partial = jnp.stack([jnp.sum(density, axis=-1), jnp.sum(density * levels, axis=-1)])
    other = lax.ppermute(partial, "band", [(0, 1), (1, 0)])
    energy_sum = partial[0] + other[0]
    moment = partial[1] + other[1]
    return sources(
        density,
        energy_sum,
        moment,
        levels,
        heading,
        ice_loss,
        sea_share,
        ice_share,
        wind_speed,
        wind_dir,
    )


def solution(mesh):
    return jax.shard_map(
        per_device,
        mesh=mesh,
        in_specs=(
            P("lat", "lon", "band"),
            P("lat", "lon"),
            P("lat", "lon"),
            P("lat", "lon"),
            P(),
            P(),
            P(None, "lat", "lon"),
            P("lat", "lon"),
            P("lat", "lon"),
            P(),
        ),
        out_specs=P("lat", "lon", "band"),
        check_vma=False,
    )
```

```python
import functools
import math

import jax
import jax.numpy as jnp
from jax import lax
from jax.experimental import pallas as pl
from jax.experimental.pallas import tpu as pltpu
from jax.sharding import PartitionSpec as P

NDIR = 36
ITERS = 4
NCOMP = 576


freq_ratio = 1.1
wind_gain = 0.12
break_coef = 0.05
south_edge = -30.0
band_span = 60.0


def quickest(behind, center, forward, beyond, courant):
    curvature = jnp.where(
        courant >= 0.0, forward - 2.0 * center + behind, beyond - 2.0 * forward + center
    )
    face_value = (
        0.5 * (center + forward)
        - 0.5 * courant * (forward - center)
        - (1.0 - courant * courant) / 6.0 * curvature
    )
    return courant * face_value


def advect(density, cell_speed, axis_dim):
    length = density.shape[axis_dim]

    def piece(array, low, high):
        return lax.slice_in_dim(array, low, high, axis=axis_dim)

    courant = 0.5 * (piece(cell_speed, 1, length - 2) + piece(cell_speed, 2, length - 1))
    fluxes = quickest(
        piece(density, 0, length - 3),
        piece(density, 1, length - 2),
        piece(density, 2, length - 1),
        piece(density, 3, length),
        courant,
    )
    faces = fluxes.shape[axis_dim]
    return piece(density, 2, length - 2) - (piece(fluxes, 1, faces) - piece(fluxes, 0, faces - 1))


def rotate(density, offset):
    dir_index = jnp.arange(density.shape[-1]) % NDIR
    target = dir_index + offset
    inner_roll = jnp.roll(density, -offset, axis=-1)
    if offset > 0:
        outer_roll = jnp.roll(density, NDIR - offset, axis=-1)
        return jnp.where(target >= NDIR, outer_roll, inner_roll)
    outer_roll = jnp.roll(density, -(offset + NDIR), axis=-1)
    return jnp.where(target < 0, outer_roll, inner_roll)


def refract(density, courant):
    fluxes = quickest(rotate(density, -1), density, rotate(density, 1), rotate(density, 2), courant)
    return density - (fluxes - rotate(fluxes, -1))


def expand(per_freq, spread):
    return jnp.dot(per_freq, spread, precision=lax.Precision.HIGHEST)


def lookup(classes, lookup_table):
    onehot = (classes[..., None] == jnp.arange(lookup_table.shape[0])).astype(jnp.float32)
    return jnp.dot(onehot, lookup_table, precision=lax.Precision.HIGHEST)


def stretch(rows, total_rows):
    latitude = (south_edge + band_span * (rows.astype(jnp.float32) + 0.5) / total_rows) * (
        math.pi / 180.0
    )
    return 1.0 / jnp.cos(latitude)


def sources(
    density,
    energy_sum,
    moment,
    levels,
    heading,
    ice_loss,
    sea_share,
    ice_share,
    wind_speed,
    wind_dir,
):
    mean_level = jnp.maximum(moment, 1.0) / jnp.maximum(energy_sum, 1.0)
    energy = energy_sum / NCOMP
    breaking = break_coef * levels * levels / mean_level[..., None] * (energy * energy)[..., None]
    growth = (
        wind_gain
        * wind_speed[..., None]
        * levels
        * jnp.maximum(jnp.cos(heading - wind_dir[..., None]), 0.0)
    )
    damping = ice_share[..., None] * ice_loss
    return sea_share[..., None] * density * jnp.exp(growth - breaking - damping)


INTERPRET = False


def face_flux(behind, center, forward, beyond, courant, weight):
    curvature = jnp.where(
        courant >= 0.0, forward - 2.0 * center + behind, beyond - 2.0 * forward + center
    )
    face_value = 0.5 * (center + forward) - 0.5 * courant * (forward - center) - weight * curvature
    return courant * face_value


def propagate_kernel(
    tab_ref, q_ref, gs_ref, tx_ref, ty_ref, st_ref, in_ref, out_ref,
    kx_ref, wx_ref, ky_ref, wy_ref, kt_ref, wt_ref, f_ref, *, width
):
    ndir, _, npos = q_ref.shape

    def pick(x, s):
        return pltpu.roll(x, (-s) % npos, 1)

    def prev(d):
        return (d + ndir - 1) % ndir

    def coefficients(d, carry):
        gs = gs_ref[...]
        ax = gs * tab_ref[0, d] * st_ref[...]
        ay = gs * tab_ref[1, d]
        kx = 0.5 * (ax + pick(ax, 1))
        ky = 0.5 * (ay + pick(ay, width))
        kt = tx_ref[...] * tab_ref[2, d] - ty_ref[...] * tab_ref[3, d]
        kx_ref[d] = kx
        ky_ref[d] = ky
        kt_ref[d] = kt
        wx_ref[d] = (1.0 - kx * kx) / 6.0
        wy_ref[d] = (1.0 - ky * ky) / 6.0
        wt_ref[d] = (1.0 - kt * kt) / 6.0
        return carry

    lax.fori_loop(0, ndir, coefficients, 0)
    inside = jnp.broadcast_to(in_ref[...] > 0.5, q_ref.shape[1:])

    def sweep(q, step, k, w):
        flux = face_flux(pick(q, -step), q, pick(q, step), pick(q, 2 * step), k, w)
        return q - (flux - pick(flux, -step))

    for substep in range(ITERS):
        source = q_ref if substep == 0 else out_ref

        def spatial(d, carry):
            q = source[d]
            if substep > 0:
                q = q - (f_ref[d] - f_ref[prev(d)])
            q = sweep(q, 1, kx_ref[d], wx_ref[d])
            q = sweep(q, width, ky_ref[d], wy_ref[d])
            out_ref[d] = jnp.where(inside, q, 0.0)
            return carry

        lax.fori_loop(0, ndir, spatial, 0)

        def directional(d, carry):
            f_ref[d] = face_flux(
                out_ref[prev(d)],
                out_ref[d],
                out_ref[(d + 1) % ndir],
                out_ref[(d + 2) % ndir],
                kt_ref[d],
                wt_ref[d],
            )
            return carry

        lax.fori_loop(0, ndir, directional, 0)

    def finish(d, carry):
        out_ref[d] = out_ref[d] - (f_ref[d] - f_ref[prev(d)])
        return carry

    lax.fori_loop(0, ndir, finish, 0)


def propagate(tables, q, gs, tx, ty, st, inside, width):
    vmem = pl.BlockSpec(memory_space=pltpu.VMEM)
    scratch = [pltpu.VMEM(q.shape, jnp.float32) for _ in range(7)]
    return pl.pallas_call(
        functools.partial(propagate_kernel, width=width),
        out_shape=jax.ShapeDtypeStruct(q.shape, jnp.float32),
        in_specs=[pl.BlockSpec(memory_space=pltpu.SMEM)] + [vmem] * 6,
        out_specs=vmem,
        scratch_shapes=scratch,
        interpret=INTERPRET,
    )(tables, q, gs, tx, ty, st, inside)


def exchange(cells, axis, dim, width, closed):
    count = lax.axis_size(axis)
    ends = count if closed else count - 1
    head = lax.slice_in_dim(cells, 0, width, axis=dim)
    tail = lax.slice_in_dim(cells, cells.shape[dim] - width, cells.shape[dim], axis=dim)
    before = lax.ppermute(tail, axis, [(i, (i + 1) % count) for i in range(ends)])
    after = lax.ppermute(head, axis, [((i + 1) % count, i) for i in range(ends)])
    return jnp.concatenate([before, cells, after], axis=dim)


def trim(array, dim, amount):
    return lax.slice_in_dim(array, amount, array.shape[dim] - amount, axis=dim)


def per_device(
    spectrum,
    sea_mask,
    ice_mask,
    depth_class,
    speed_table,
    refraction_table,
    depth_slope,
    wind_speed,
    wind_dir,
    ice_rate,
):
    rows_dev, cols_dev, comps_dev = spectrum.shape
    freqs_dev = comps_dev // NDIR
    halo = 2 * ITERS
    band_index = lax.axis_index("band")
    first_comp = band_index * comps_dev
    local_comp = jnp.arange(comps_dev)
    comp_index = first_comp + local_comp
    spread = (local_comp[None, :] // NDIR == jnp.arange(freqs_dev)[:, None]).astype(jnp.float32)
    heading = 2.0 * math.pi * (comp_index % NDIR).astype(jnp.float32) / NDIR
    face_angle = heading + math.pi / NDIR
    cos_head = jnp.cos(heading)
    sin_head = jnp.sin(heading)
    sin_face = jnp.sin(face_angle)
    cos_face = jnp.cos(face_angle)
    sea_share = sea_mask.astype(jnp.float32)
    ice_share = ice_mask.astype(jnp.float32)
    speed_local = lax.dynamic_slice_in_dim(speed_table, band_index * freqs_dev, freqs_dev, 1)
    refr_local = lax.dynamic_slice_in_dim(refraction_table, band_index * freqs_dev, freqs_dev, 1)
    group_speed = lookup(depth_class, speed_local) * sea_share[..., None]
    turning = lookup(depth_class, refr_local) * sea_share[..., None]
    turn_x = turning * depth_slope[0][..., None]
    turn_y = turning * depth_slope[1][..., None]
    density = spectrum * sea_share[..., None]

    stacked = jnp.concatenate([density, group_speed, turn_x, turn_y], axis=-1)
    stacked = exchange(exchange(stacked, "lon", 1, halo, True), "lat", 0, halo, False)
    density = stacked[..., :comps_dev]
    fields = stacked[..., comps_dev:]

    total_rows = rows_dev * lax.axis_size("lat")
    first_row = lax.axis_index("lat") * rows_dev - halo
    rows_ext, cols_ext = stacked.shape[:2]
    rows_at = first_row + jnp.arange(rows_ext)
    inside = ((rows_at >= 0) & (rows_at < total_rows)).astype(jnp.float32)
    positions = rows_ext * cols_ext
    per_pos = lambda v: jnp.repeat(v, cols_ext).reshape(1, positions)
    tables = jnp.stack([cos_head, sin_head, sin_face, cos_face])[:, :NDIR]
    by_dir = density.reshape(positions, freqs_dev, NDIR).transpose(2, 1, 0)
    by_freq = [
        fields[..., i * freqs_dev : (i + 1) * freqs_dev].reshape(positions, freqs_dev).T
        for i in range(3)
    ]
    moved = propagate(
        tables, by_dir, *by_freq, per_pos(stretch(rows_at, total_rows)), per_pos(inside), cols_ext
    )
    density = moved.transpose(2, 1, 0).reshape(rows_ext, cols_ext, comps_dev)
    density = density[halo : halo + rows_dev, halo : halo + cols_dev]

    levels = jnp.exp(math.log(freq_ratio) * (comp_index // NDIR).astype(jnp.float32))
    ice_loss = lax.dynamic_slice_in_dim(jnp.repeat(ice_rate, NDIR), first_comp, comps_dev, 0)
    partial = jnp.stack([jnp.sum(density, axis=-1), jnp.sum(density * levels, axis=-1)])
    other = lax.ppermute(partial, "band", [(0, 1), (1, 0)])
    energy_sum = partial[0] + other[0]
    moment = partial[1] + other[1]
    return sources(
        density,
        energy_sum,
        moment,
        levels,
        heading,
        ice_loss,
        sea_share,
        ice_share,
        wind_speed,
        wind_dir,
    )


def solution(mesh):
    return jax.shard_map(
        per_device,
        mesh=mesh,
        in_specs=(
            P("lat", "lon", "band"),
            P("lat", "lon"),
            P("lat", "lon"),
            P("lat", "lon"),
            P(),
            P(),
            P(None, "lat", "lon"),
            P("lat", "lon"),
            P("lat", "lon"),
            P(),
        ),
        out_specs=P("lat", "lon", "band"),
        check_vma=False,
    )
```

```python
import functools
import math

import jax
import jax.numpy as jnp
from jax import lax
from jax.experimental import pallas as pl
from jax.experimental.pallas import tpu as pltpu
from jax.sharding import PartitionSpec as P

NDIR = 36
ITERS = 4
NCOMP = 576


freq_ratio = 1.1
wind_gain = 0.12
break_coef = 0.05
south_edge = -30.0
band_span = 60.0


def quickest(behind, center, forward, beyond, courant):
    curvature = jnp.where(
        courant >= 0.0, forward - 2.0 * center + behind, beyond - 2.0 * forward + center
    )
    face_value = (
        0.5 * (center + forward)
        - 0.5 * courant * (forward - center)
        - (1.0 - courant * courant) / 6.0 * curvature
    )
    return courant * face_value


def advect(density, cell_speed, axis_dim):
    length = density.shape[axis_dim]

    def piece(array, low, high):
        return lax.slice_in_dim(array, low, high, axis=axis_dim)

    courant = 0.5 * (piece(cell_speed, 1, length - 2) + piece(cell_speed, 2, length - 1))
    fluxes = quickest(
        piece(density, 0, length - 3),
        piece(density, 1, length - 2),
        piece(density, 2, length - 1),
        piece(density, 3, length),
        courant,
    )
    faces = fluxes.shape[axis_dim]
    return piece(density, 2, length - 2) - (piece(fluxes, 1, faces) - piece(fluxes, 0, faces - 1))


def rotate(density, offset):
    dir_index = jnp.arange(density.shape[-1]) % NDIR
    target = dir_index + offset
    inner_roll = jnp.roll(density, -offset, axis=-1)
    if offset > 0:
        outer_roll = jnp.roll(density, NDIR - offset, axis=-1)
        return jnp.where(target >= NDIR, outer_roll, inner_roll)
    outer_roll = jnp.roll(density, -(offset + NDIR), axis=-1)
    return jnp.where(target < 0, outer_roll, inner_roll)


def refract(density, courant):
    fluxes = quickest(rotate(density, -1), density, rotate(density, 1), rotate(density, 2), courant)
    return density - (fluxes - rotate(fluxes, -1))


def expand(per_freq, spread):
    return jnp.dot(per_freq, spread, precision=lax.Precision.HIGHEST)


def lookup(classes, lookup_table):
    onehot = (classes[..., None] == jnp.arange(lookup_table.shape[0])).astype(jnp.float32)
    return jnp.dot(onehot, lookup_table, precision=lax.Precision.HIGHEST)


def stretch(rows, total_rows):
    latitude = (south_edge + band_span * (rows.astype(jnp.float32) + 0.5) / total_rows) * (
        math.pi / 180.0
    )
    return 1.0 / jnp.cos(latitude)


def sources(
    density,
    energy_sum,
    moment,
    levels,
    heading,
    ice_loss,
    sea_share,
    ice_share,
    wind_speed,
    wind_dir,
):
    mean_level = jnp.maximum(moment, 1.0) / jnp.maximum(energy_sum, 1.0)
    energy = energy_sum / NCOMP
    breaking = break_coef * levels * levels / mean_level[..., None] * (energy * energy)[..., None]
    growth = (
        wind_gain
        * wind_speed[..., None]
        * levels
        * jnp.maximum(jnp.cos(heading - wind_dir[..., None]), 0.0)
    )
    damping = ice_share[..., None] * ice_loss
    return sea_share[..., None] * density * jnp.exp(growth - breaking - damping)


INTERPRET = False
MESH_ID = pl.DeviceIdType.MESH
OFFSETS = [(a, b) for a in (-1, 0, 1) for b in (-1, 0, 1) if (a, b) != (0, 0)]


def halo_kernel(in_ref, out_ref, send_sem, recv_sem, *, halo):
    lon = lax.axis_index("lon")
    lat = lax.axis_index("lat")
    nlon = lax.axis_size("lon")
    nlat = lax.axis_size("lat")
    rows, cols = in_ref.shape[:2]

    def target(a, b):
        return {"lon": lax.rem(lon + b + nlon, nlon), "lat": lat + a}

    def has(a):
        return jnp.logical_and(lat + a >= 0, lat + a < nlat)

    def span(a, size):
        if a == 1:
            return pl.ds(size - halo, halo), pl.ds(0, halo)
        if a == -1:
            return pl.ds(0, halo), pl.ds(size + halo, halo)
        return pl.ds(0, size), pl.ds(halo, size)

    barrier = pltpu.get_barrier_semaphore()
    for a, b in OFFSETS:

        @pl.when(has(a))
        def _():
            pl.semaphore_signal(barrier, inc=1, device_id=target(a, b), device_id_type=MESH_ID)

    below = (lat + nlat - 1) // nlat
    above = 1 - lat // (nlat - 1)
    pl.semaphore_wait(barrier, 3 * (1 + below + above) - 1)

    copies = []
    for k, (a, b) in enumerate(OFFSETS):
        rows_src, rows_dst = span(a, rows)
        cols_src, cols_dst = span(b, cols)
        copy = pltpu.make_async_remote_copy(
            src_ref=in_ref.at[rows_src, cols_src],
            dst_ref=out_ref.at[rows_dst, cols_dst],
            send_sem=send_sem.at[k],
            recv_sem=recv_sem.at[k],
            device_id=target(a, b),
            device_id_type=MESH_ID,
        )
        pl.when(has(a))(copy.start)
        copies.append((a, copy))

    out_ref[pl.ds(halo, rows), pl.ds(halo, cols)] = in_ref[...]
    ghost = jnp.zeros((halo,) + out_ref.shape[1:], out_ref.dtype)

    @pl.when(lat == 0)
    def _():
        out_ref[pl.ds(0, halo)] = ghost

    @pl.when(lat == nlat - 1)
    def _():
        out_ref[pl.ds(rows + halo, halo)] = ghost

    for a, copy in copies:
        pl.when(has(a))(copy.wait_send)
        pl.when(has(-a))(copy.wait_recv)


def halo_exchange(cells, halo):
    rows, cols, chans = cells.shape
    vmem = pl.BlockSpec(memory_space=pltpu.VMEM)
    return pl.pallas_call(
        functools.partial(halo_kernel, halo=halo),
        out_shape=jax.ShapeDtypeStruct((rows + 2 * halo, cols + 2 * halo, chans), cells.dtype),
        in_specs=[vmem],
        out_specs=vmem,
        scratch_shapes=[pltpu.SemaphoreType.DMA((8,)), pltpu.SemaphoreType.DMA((8,))],
        compiler_params=pltpu.CompilerParams(collective_id=0, has_side_effects=True),
        interpret=pltpu.InterpretParams(detect_races=True) if INTERPRET else False,
    )(cells)


def exchange(cells, axis, dim, width, closed):
    count = lax.axis_size(axis)
    ends = count if closed else count - 1
    head = lax.slice_in_dim(cells, 0, width, axis=dim)
    tail = lax.slice_in_dim(cells, cells.shape[dim] - width, cells.shape[dim], axis=dim)
    before = lax.ppermute(tail, axis, [(i, (i + 1) % count) for i in range(ends)])
    after = lax.ppermute(head, axis, [((i + 1) % count, i) for i in range(ends)])
    return jnp.concatenate([before, cells, after], axis=dim)


def trim(array, dim, amount):
    return lax.slice_in_dim(array, amount, array.shape[dim] - amount, axis=dim)


def per_device(
    spectrum,
    sea_mask,
    ice_mask,
    depth_class,
    speed_table,
    refraction_table,
    depth_slope,
    wind_speed,
    wind_dir,
    ice_rate,
):
    rows_dev, cols_dev, comps_dev = spectrum.shape
    freqs_dev = comps_dev // NDIR
    halo = 2 * ITERS
    band_index = lax.axis_index("band")
    first_comp = band_index * comps_dev
    local_comp = jnp.arange(comps_dev)
    comp_index = first_comp + local_comp
    spread = (local_comp[None, :] // NDIR == jnp.arange(freqs_dev)[:, None]).astype(jnp.float32)
    heading = 2.0 * math.pi * (comp_index % NDIR).astype(jnp.float32) / NDIR
    face_angle = heading + math.pi / NDIR
    cos_head = jnp.cos(heading)
    sin_head = jnp.sin(heading)
    sin_face = jnp.sin(face_angle)
    cos_face = jnp.cos(face_angle)
    sea_share = sea_mask.astype(jnp.float32)
    ice_share = ice_mask.astype(jnp.float32)
    speed_local = lax.dynamic_slice_in_dim(speed_table, band_index * freqs_dev, freqs_dev, 1)
    refr_local = lax.dynamic_slice_in_dim(refraction_table, band_index * freqs_dev, freqs_dev, 1)
    group_speed = lookup(depth_class, speed_local) * sea_share[..., None]
    turning = lookup(depth_class, refr_local) * sea_share[..., None]
    turn_x = turning * depth_slope[0][..., None]
    turn_y = turning * depth_slope[1][..., None]
    density = spectrum * sea_share[..., None]

    stacked = jnp.concatenate([density, group_speed, turn_x, turn_y], axis=-1)
    stacked = halo_exchange(stacked, halo)
    density = stacked[..., :comps_dev]
    fields = stacked[..., comps_dev:]

    total_rows = rows_dev * lax.axis_size("lat")
    first_row = lax.axis_index("lat") * rows_dev - halo
    rows_ext = first_row + jnp.arange(rows_dev + 2 * halo)
    inside = ((rows_ext >= 0) & (rows_ext < total_rows))[:, None, None]
    stretch_rows = stretch(rows_ext, total_rows)
    gs_ext = expand(fields[..., :freqs_dev], spread)
    along_x = gs_ext * cos_head * stretch_rows[:, None, None]
    along_y = gs_ext * sin_head
    along_t = (
        expand(fields[..., freqs_dev : 2 * freqs_dev], spread) * sin_face
        - expand(fields[..., 2 * freqs_dev :], spread) * cos_face
    )
    for substep in range(ITERS):
        density = advect(density, along_x, 1)
        along_x, along_y, along_t = [trim(a, 1, 2) for a in (along_x, along_y, along_t)]
        density = advect(density, along_y, 0)
        inside = trim(inside, 0, 2)
        density = jnp.where(inside, density, 0.0)
        along_x, along_y, along_t = [trim(a, 0, 2) for a in (along_x, along_y, along_t)]
        density = refract(density, along_t)

    levels = jnp.exp(math.log(freq_ratio) * (comp_index // NDIR).astype(jnp.float32))
    ice_loss = lax.dynamic_slice_in_dim(jnp.repeat(ice_rate, NDIR), first_comp, comps_dev, 0)
    partial = jnp.stack([jnp.sum(density, axis=-1), jnp.sum(density * levels, axis=-1)])
    other = lax.ppermute(partial, "band", [(0, 1), (1, 0)])
    energy_sum = partial[0] + other[0]
    moment = partial[1] + other[1]
    return sources(
        density,
        energy_sum,
        moment,
        levels,
        heading,
        ice_loss,
        sea_share,
        ice_share,
        wind_speed,
        wind_dir,
    )


def solution(mesh):
    return jax.shard_map(
        per_device,
        mesh=mesh,
        in_specs=(
            P("lat", "lon", "band"),
            P("lat", "lon"),
            P("lat", "lon"),
            P("lat", "lon"),
            P(),
            P(),
            P(None, "lat", "lon"),
            P("lat", "lon"),
            P("lat", "lon"),
            P(),
        ),
        out_specs=P("lat", "lon", "band"),
        check_vma=False,
    )
```

```python
import functools
import math

import jax
import jax.numpy as jnp
from jax import lax
from jax.experimental import pallas as pl
from jax.experimental.pallas import tpu as pltpu
from jax.sharding import PartitionSpec as P

NDIR = 36
ITERS = 4
NCOMP = 576


freq_ratio = 1.1
wind_gain = 0.12
break_coef = 0.05
south_edge = -30.0
band_span = 60.0


def quickest(behind, center, forward, beyond, courant):
    curvature = jnp.where(
        courant >= 0.0, forward - 2.0 * center + behind, beyond - 2.0 * forward + center
    )
    face_value = (
        0.5 * (center + forward)
        - 0.5 * courant * (forward - center)
        - (1.0 - courant * courant) / 6.0 * curvature
    )
    return courant * face_value


def advect(density, cell_speed, axis_dim):
    length = density.shape[axis_dim]

    def piece(array, low, high):
        return lax.slice_in_dim(array, low, high, axis=axis_dim)

    courant = 0.5 * (piece(cell_speed, 1, length - 2) + piece(cell_speed, 2, length - 1))
    fluxes = quickest(
        piece(density, 0, length - 3),
        piece(density, 1, length - 2),
        piece(density, 2, length - 1),
        piece(density, 3, length),
        courant,
    )
    faces = fluxes.shape[axis_dim]
    return piece(density, 2, length - 2) - (piece(fluxes, 1, faces) - piece(fluxes, 0, faces - 1))


def rotate(density, offset):
    dir_index = jnp.arange(density.shape[-1]) % NDIR
    target = dir_index + offset
    inner_roll = jnp.roll(density, -offset, axis=-1)
    if offset > 0:
        outer_roll = jnp.roll(density, NDIR - offset, axis=-1)
        return jnp.where(target >= NDIR, outer_roll, inner_roll)
    outer_roll = jnp.roll(density, -(offset + NDIR), axis=-1)
    return jnp.where(target < 0, outer_roll, inner_roll)


def refract(density, courant):
    fluxes = quickest(rotate(density, -1), density, rotate(density, 1), rotate(density, 2), courant)
    return density - (fluxes - rotate(fluxes, -1))


def expand(per_freq, spread):
    return jnp.dot(per_freq, spread, precision=lax.Precision.HIGHEST)


def lookup(classes, lookup_table):
    onehot = (classes[..., None] == jnp.arange(lookup_table.shape[0])).astype(jnp.float32)
    return jnp.dot(onehot, lookup_table, precision=lax.Precision.HIGHEST)


def stretch(rows, total_rows):
    latitude = (south_edge + band_span * (rows.astype(jnp.float32) + 0.5) / total_rows) * (
        math.pi / 180.0
    )
    return 1.0 / jnp.cos(latitude)


def sources(
    density,
    energy_sum,
    moment,
    levels,
    heading,
    ice_loss,
    sea_share,
    ice_share,
    wind_speed,
    wind_dir,
):
    mean_level = jnp.maximum(moment, 1.0) / jnp.maximum(energy_sum, 1.0)
    energy = energy_sum / NCOMP
    breaking = break_coef * levels * levels / mean_level[..., None] * (energy * energy)[..., None]
    growth = (
        wind_gain
        * wind_speed[..., None]
        * levels
        * jnp.maximum(jnp.cos(heading - wind_dir[..., None]), 0.0)
    )
    damping = ice_share[..., None] * ice_loss
    return sea_share[..., None] * density * jnp.exp(growth - breaking - damping)


INTERPRET = False
MESH_ID = pl.DeviceIdType.MESH
OFFSETS = [(a, b) for a in (-1, 0, 1) for b in (-1, 0, 1) if (a, b) != (0, 0)]


def halo_kernel(in_ref, out_ref, send_sem, recv_sem, *, halo):
    lon = lax.axis_index("lon")
    lat = lax.axis_index("lat")
    nlon = lax.axis_size("lon")
    nlat = lax.axis_size("lat")
    rows, cols = in_ref.shape[:2]

    def target(a, b):
        return {"lon": lax.rem(lon + b + nlon, nlon), "lat": lat + a}

    def has(a):
        return jnp.logical_and(lat + a >= 0, lat + a < nlat)

    def span(a, size):
        if a == 1:
            return pl.ds(size - halo, halo), pl.ds(0, halo)
        if a == -1:
            return pl.ds(0, halo), pl.ds(size + halo, halo)
        return pl.ds(0, size), pl.ds(halo, size)

    barrier = pltpu.get_barrier_semaphore()
    for a, b in OFFSETS:

        @pl.when(has(a))
        def _():
            pl.semaphore_signal(barrier, inc=1, device_id=target(a, b), device_id_type=MESH_ID)

    below = (lat + nlat - 1) // nlat
    above = 1 - lat // (nlat - 1)
    pl.semaphore_wait(barrier, 3 * (1 + below + above) - 1)

    copies = []
    for k, (a, b) in enumerate(OFFSETS):
        rows_src, rows_dst = span(a, rows)
        cols_src, cols_dst = span(b, cols)
        copy = pltpu.make_async_remote_copy(
            src_ref=in_ref.at[rows_src, cols_src],
            dst_ref=out_ref.at[rows_dst, cols_dst],
            send_sem=send_sem.at[k],
            recv_sem=recv_sem.at[k],
            device_id=target(a, b),
            device_id_type=MESH_ID,
        )
        pl.when(has(a))(copy.start)
        copies.append((a, copy))

    out_ref[pl.ds(halo, rows), pl.ds(halo, cols)] = in_ref[...]
    ghost = jnp.zeros((halo,) + out_ref.shape[1:], out_ref.dtype)

    @pl.when(lat == 0)
    def _():
        out_ref[pl.ds(0, halo)] = ghost

    @pl.when(lat == nlat - 1)
    def _():
        out_ref[pl.ds(rows + halo, halo)] = ghost

    for a, copy in copies:
        pl.when(has(a))(copy.wait_send)
        pl.when(has(-a))(copy.wait_recv)


def halo_exchange(cells, halo):
    rows, cols, chans = cells.shape
    vmem = pl.BlockSpec(memory_space=pltpu.VMEM)
    return pl.pallas_call(
        functools.partial(halo_kernel, halo=halo),
        out_shape=jax.ShapeDtypeStruct((rows + 2 * halo, cols + 2 * halo, chans), cells.dtype),
        in_specs=[vmem],
        out_specs=vmem,
        scratch_shapes=[pltpu.SemaphoreType.DMA((8,)), pltpu.SemaphoreType.DMA((8,))],
        compiler_params=pltpu.CompilerParams(collective_id=0, has_side_effects=True),
        interpret=pltpu.InterpretParams(detect_races=True) if INTERPRET else False,
    )(cells)


def exchange(cells, axis, dim, width, closed):
    count = lax.axis_size(axis)
    ends = count if closed else count - 1
    head = lax.slice_in_dim(cells, 0, width, axis=dim)
    tail = lax.slice_in_dim(cells, cells.shape[dim] - width, cells.shape[dim], axis=dim)
    before = lax.ppermute(tail, axis, [(i, (i + 1) % count) for i in range(ends)])
    after = lax.ppermute(head, axis, [((i + 1) % count, i) for i in range(ends)])
    return jnp.concatenate([before, cells, after], axis=dim)


def trim(array, dim, amount):
    return lax.slice_in_dim(array, amount, array.shape[dim] - amount, axis=dim)


def per_device(
    spectrum,
    sea_mask,
    ice_mask,
    depth_class,
    speed_table,
    refraction_table,
    depth_slope,
    wind_speed,
    wind_dir,
    ice_rate,
):
    rows_dev, cols_dev, comps_dev = spectrum.shape
    freqs_dev = comps_dev // NDIR
    halo = 2 * ITERS
    band_index = lax.axis_index("band")
    first_comp = band_index * comps_dev
    local_comp = jnp.arange(comps_dev)
    comp_index = first_comp + local_comp
    spread = (local_comp[None, :] // NDIR == jnp.arange(freqs_dev)[:, None]).astype(jnp.float32)
    heading = 2.0 * math.pi * (comp_index % NDIR).astype(jnp.float32) / NDIR
    face_angle = heading + math.pi / NDIR
    cos_head = jnp.cos(heading)
    sin_head = jnp.sin(heading)
    sin_face = jnp.sin(face_angle)
    cos_face = jnp.cos(face_angle)
    sea_share = sea_mask.astype(jnp.float32)
    ice_share = ice_mask.astype(jnp.float32)
    speed_local = lax.dynamic_slice_in_dim(speed_table, band_index * freqs_dev, freqs_dev, 1)
    refr_local = lax.dynamic_slice_in_dim(refraction_table, band_index * freqs_dev, freqs_dev, 1)
    chosen = (depth_class[..., None] == jnp.arange(speed_table.shape[0]))[..., None]
    group_speed = jnp.sum(jnp.where(chosen, speed_local, 0.0), axis=2) * sea_share[..., None]
    turning = jnp.sum(jnp.where(chosen, refr_local, 0.0), axis=2) * sea_share[..., None]
    turn_x = turning * depth_slope[0][..., None]
    turn_y = turning * depth_slope[1][..., None]
    density = spectrum * sea_share[..., None]

    stacked = jnp.concatenate([density, group_speed, turn_x, turn_y], axis=-1)
    stacked = halo_exchange(stacked, halo)
    density = stacked[..., :comps_dev]
    fields = stacked[..., comps_dev:]

    total_rows = rows_dev * lax.axis_size("lat")
    first_row = lax.axis_index("lat") * rows_dev - halo
    rows_ext = first_row + jnp.arange(rows_dev + 2 * halo)
    inside = ((rows_ext >= 0) & (rows_ext < total_rows))[:, None, None]
    stretch_rows = stretch(rows_ext, total_rows)
    gs_ext = expand(fields[..., :freqs_dev], spread)
    along_x = gs_ext * cos_head * stretch_rows[:, None, None]
    along_y = gs_ext * sin_head
    along_t = (
        expand(fields[..., freqs_dev : 2 * freqs_dev], spread) * sin_face
        - expand(fields[..., 2 * freqs_dev :], spread) * cos_face
    )
    for substep in range(ITERS):
        density = advect(density, along_x, 1)
        along_x, along_y, along_t = [trim(a, 1, 2) for a in (along_x, along_y, along_t)]
        density = advect(density, along_y, 0)
        inside = trim(inside, 0, 2)
        density = jnp.where(inside, density, 0.0)
        along_x, along_y, along_t = [trim(a, 0, 2) for a in (along_x, along_y, along_t)]
        density = refract(density, along_t)

    levels = jnp.exp(math.log(freq_ratio) * (comp_index // NDIR).astype(jnp.float32))
    ice_loss = lax.dynamic_slice_in_dim(jnp.repeat(ice_rate, NDIR), first_comp, comps_dev, 0)
    partial = jnp.stack([jnp.sum(density, axis=-1), jnp.sum(density * levels, axis=-1)])
    other = lax.ppermute(partial, "band", [(0, 1), (1, 0)])
    energy_sum = partial[0] + other[0]
    moment = partial[1] + other[1]
    return sources(
        density,
        energy_sum,
        moment,
        levels,
        heading,
        ice_loss,
        sea_share,
        ice_share,
        wind_speed,
        wind_dir,
    )


def solution(mesh):
    return jax.shard_map(
        per_device,
        mesh=mesh,
        in_specs=(
            P("lat", "lon", "band"),
            P("lat", "lon"),
            P("lat", "lon"),
            P("lat", "lon"),
            P(),
            P(),
            P(None, "lat", "lon"),
            P("lat", "lon"),
            P("lat", "lon"),
            P(),
        ),
        out_specs=P("lat", "lon", "band"),
        check_vma=False,
    )
```

```python
import functools
import math

import jax
import jax.numpy as jnp
from jax import lax
from jax.experimental import pallas as pl
from jax.experimental.pallas import tpu as pltpu
from jax.sharding import PartitionSpec as P

NDIR = 36
ITERS = 4
NCOMP = 576


freq_ratio = 1.1
wind_gain = 0.12
break_coef = 0.05
south_edge = -30.0
band_span = 60.0


def quickest(behind, center, forward, beyond, courant):
    curvature = jnp.where(
        courant >= 0.0, forward - 2.0 * center + behind, beyond - 2.0 * forward + center
    )
    face_value = (
        0.5 * (center + forward)
        - 0.5 * courant * (forward - center)
        - (1.0 - courant * courant) / 6.0 * curvature
    )
    return courant * face_value


def advect(density, cell_speed, axis_dim):
    length = density.shape[axis_dim]

    def piece(array, low, high):
        return lax.slice_in_dim(array, low, high, axis=axis_dim)

    courant = 0.5 * (piece(cell_speed, 1, length - 2) + piece(cell_speed, 2, length - 1))
    fluxes = quickest(
        piece(density, 0, length - 3),
        piece(density, 1, length - 2),
        piece(density, 2, length - 1),
        piece(density, 3, length),
        courant,
    )
    faces = fluxes.shape[axis_dim]
    return piece(density, 2, length - 2) - (piece(fluxes, 1, faces) - piece(fluxes, 0, faces - 1))


def rotate(density, offset):
    dir_index = jnp.arange(density.shape[-1]) % NDIR
    target = dir_index + offset
    inner_roll = jnp.roll(density, -offset, axis=-1)
    if offset > 0:
        outer_roll = jnp.roll(density, NDIR - offset, axis=-1)
        return jnp.where(target >= NDIR, outer_roll, inner_roll)
    outer_roll = jnp.roll(density, -(offset + NDIR), axis=-1)
    return jnp.where(target < 0, outer_roll, inner_roll)


def refract(density, courant):
    fluxes = quickest(rotate(density, -1), density, rotate(density, 1), rotate(density, 2), courant)
    return density - (fluxes - rotate(fluxes, -1))


def expand(per_freq, spread):
    return jnp.dot(per_freq, spread, precision=lax.Precision.HIGHEST)


def lookup(classes, lookup_table):
    onehot = (classes[..., None] == jnp.arange(lookup_table.shape[0])).astype(jnp.float32)
    return jnp.dot(onehot, lookup_table, precision=lax.Precision.HIGHEST)


def stretch(rows, total_rows):
    latitude = (south_edge + band_span * (rows.astype(jnp.float32) + 0.5) / total_rows) * (
        math.pi / 180.0
    )
    return 1.0 / jnp.cos(latitude)


def sources(
    density,
    energy_sum,
    moment,
    levels,
    heading,
    ice_loss,
    sea_share,
    ice_share,
    wind_speed,
    wind_dir,
):
    mean_level = jnp.maximum(moment, 1.0) / jnp.maximum(energy_sum, 1.0)
    energy = energy_sum / NCOMP
    breaking = break_coef * levels * levels / mean_level[..., None] * (energy * energy)[..., None]
    growth = (
        wind_gain
        * wind_speed[..., None]
        * levels
        * jnp.maximum(jnp.cos(heading - wind_dir[..., None]), 0.0)
    )
    damping = ice_share[..., None] * ice_loss
    return sea_share[..., None] * density * jnp.exp(growth - breaking - damping)


INTERPRET = False
MESH_ID = pl.DeviceIdType.MESH
OFFSETS = [(a, b) for a in (-1, 0, 1) for b in (-1, 0, 1) if (a, b) != (0, 0)]


def halo_kernel(in_ref, out_ref, send_sem, recv_sem, *, halo):
    lon = lax.axis_index("lon")
    lat = lax.axis_index("lat")
    nlon = lax.axis_size("lon")
    nlat = lax.axis_size("lat")
    rows, cols = in_ref.shape[:2]

    def target(a, b):
        return {"lon": lax.rem(lon + b + nlon, nlon), "lat": lat + a}

    def has(a):
        return jnp.logical_and(lat + a >= 0, lat + a < nlat)

    def span(a, size):
        if a == 1:
            return pl.ds(size - halo, halo), pl.ds(0, halo)
        if a == -1:
            return pl.ds(0, halo), pl.ds(size + halo, halo)
        return pl.ds(0, size), pl.ds(halo, size)

    barrier = pltpu.get_barrier_semaphore()
    for a, b in OFFSETS:

        @pl.when(has(a))
        def _():
            pl.semaphore_signal(barrier, inc=1, device_id=target(a, b), device_id_type=MESH_ID)

    below = (lat + nlat - 1) // nlat
    above = 1 - lat // (nlat - 1)
    pl.semaphore_wait(barrier, 3 * (1 + below + above) - 1)

    copies = []
    for k, (a, b) in enumerate(OFFSETS):
        rows_src, rows_dst = span(a, rows)
        cols_src, cols_dst = span(b, cols)
        copy = pltpu.make_async_remote_copy(
            src_ref=in_ref.at[rows_src, cols_src],
            dst_ref=out_ref.at[rows_dst, cols_dst],
            send_sem=send_sem.at[k],
            recv_sem=recv_sem.at[k],
            device_id=target(a, b),
            device_id_type=MESH_ID,
        )
        pl.when(has(a))(copy.start)
        copies.append((a, copy))

    out_ref[pl.ds(halo, rows), pl.ds(halo, cols)] = in_ref[...]
    ghost = jnp.zeros((halo,) + out_ref.shape[1:], out_ref.dtype)

    @pl.when(lat == 0)
    def _():
        out_ref[pl.ds(0, halo)] = ghost

    @pl.when(lat == nlat - 1)
    def _():
        out_ref[pl.ds(rows + halo, halo)] = ghost

    for a, copy in copies:
        pl.when(has(a))(copy.wait_send)
        pl.when(has(-a))(copy.wait_recv)


def halo_exchange(cells, halo):
    rows, cols, chans = cells.shape
    vmem = pl.BlockSpec(memory_space=pltpu.VMEM)
    return pl.pallas_call(
        functools.partial(halo_kernel, halo=halo),
        out_shape=jax.ShapeDtypeStruct((rows + 2 * halo, cols + 2 * halo, chans), cells.dtype),
        in_specs=[vmem],
        out_specs=vmem,
        scratch_shapes=[pltpu.SemaphoreType.DMA((8,)), pltpu.SemaphoreType.DMA((8,))],
        compiler_params=pltpu.CompilerParams(collective_id=0, has_side_effects=True),
        interpret=pltpu.InterpretParams(detect_races=True) if INTERPRET else False,
    )(cells)


def swap_kernel(in_ref, out_ref, send_sem, recv_sem):
    peer = {"band": 1 - lax.axis_index("band")}
    barrier = pltpu.get_barrier_semaphore()
    pl.semaphore_signal(barrier, inc=1, device_id=peer, device_id_type=MESH_ID)
    pl.semaphore_wait(barrier, 1)
    copy = pltpu.make_async_remote_copy(
        src_ref=in_ref,
        dst_ref=out_ref,
        send_sem=send_sem,
        recv_sem=recv_sem,
        device_id=peer,
        device_id_type=MESH_ID,
    )
    copy.start()
    copy.wait()


def band_swap(values):
    vmem = pl.BlockSpec(memory_space=pltpu.VMEM)
    return pl.pallas_call(
        swap_kernel,
        out_shape=jax.ShapeDtypeStruct(values.shape, values.dtype),
        in_specs=[vmem],
        out_specs=vmem,
        scratch_shapes=[pltpu.SemaphoreType.DMA(()), pltpu.SemaphoreType.DMA(())],
        compiler_params=pltpu.CompilerParams(collective_id=1, has_side_effects=True),
        interpret=pltpu.InterpretParams(detect_races=True) if INTERPRET else False,
    )(values)


def exchange(cells, axis, dim, width, closed):
    count = lax.axis_size(axis)
    ends = count if closed else count - 1
    head = lax.slice_in_dim(cells, 0, width, axis=dim)
    tail = lax.slice_in_dim(cells, cells.shape[dim] - width, cells.shape[dim], axis=dim)
    before = lax.ppermute(tail, axis, [(i, (i + 1) % count) for i in range(ends)])
    after = lax.ppermute(head, axis, [((i + 1) % count, i) for i in range(ends)])
    return jnp.concatenate([before, cells, after], axis=dim)


def trim(array, dim, amount):
    return lax.slice_in_dim(array, amount, array.shape[dim] - amount, axis=dim)


def per_device(
    spectrum,
    sea_mask,
    ice_mask,
    depth_class,
    speed_table,
    refraction_table,
    depth_slope,
    wind_speed,
    wind_dir,
    ice_rate,
):
    rows_dev, cols_dev, comps_dev = spectrum.shape
    freqs_dev = comps_dev // NDIR
    halo = 2 * ITERS
    band_index = lax.axis_index("band")
    first_comp = band_index * comps_dev
    local_comp = jnp.arange(comps_dev)
    comp_index = first_comp + local_comp
    spread = (local_comp[None, :] // NDIR == jnp.arange(freqs_dev)[:, None]).astype(jnp.float32)
    heading = 2.0 * math.pi * (comp_index % NDIR).astype(jnp.float32) / NDIR
    face_angle = heading + math.pi / NDIR
    cos_head = jnp.cos(heading)
    sin_head = jnp.sin(heading)
    sin_face = jnp.sin(face_angle)
    cos_face = jnp.cos(face_angle)
    sea_share = sea_mask.astype(jnp.float32)
    ice_share = ice_mask.astype(jnp.float32)
    speed_local = lax.dynamic_slice_in_dim(speed_table, band_index * freqs_dev, freqs_dev, 1)
    refr_local = lax.dynamic_slice_in_dim(refraction_table, band_index * freqs_dev, freqs_dev, 1)
    chosen = (depth_class[..., None] == jnp.arange(speed_table.shape[0]))[..., None]
    group_speed = jnp.sum(jnp.where(chosen, speed_local, 0.0), axis=2) * sea_share[..., None]
    turning = jnp.sum(jnp.where(chosen, refr_local, 0.0), axis=2) * sea_share[..., None]
    turn_x = turning * depth_slope[0][..., None]
    turn_y = turning * depth_slope[1][..., None]
    density = spectrum * sea_share[..., None]

    stacked = jnp.concatenate([density, group_speed, turn_x, turn_y], axis=-1)
    stacked = halo_exchange(stacked, halo)
    density = stacked[..., :comps_dev]
    fields = stacked[..., comps_dev:]

    total_rows = rows_dev * lax.axis_size("lat")
    first_row = lax.axis_index("lat") * rows_dev - halo
    rows_ext = first_row + jnp.arange(rows_dev + 2 * halo)
    inside = ((rows_ext >= 0) & (rows_ext < total_rows))[:, None, None]
    stretch_rows = stretch(rows_ext, total_rows)
    gs_ext = expand(fields[..., :freqs_dev], spread)
    along_x = gs_ext * cos_head * stretch_rows[:, None, None]
    along_y = gs_ext * sin_head
    along_t = (
        expand(fields[..., freqs_dev : 2 * freqs_dev], spread) * sin_face
        - expand(fields[..., 2 * freqs_dev :], spread) * cos_face
    )
    for substep in range(ITERS):
        density = advect(density, along_x, 1)
        along_x, along_y, along_t = [trim(a, 1, 2) for a in (along_x, along_y, along_t)]
        density = advect(density, along_y, 0)
        inside = trim(inside, 0, 2)
        density = jnp.where(inside, density, 0.0)
        along_x, along_y, along_t = [trim(a, 0, 2) for a in (along_x, along_y, along_t)]
        density = refract(density, along_t)

    levels = jnp.exp(math.log(freq_ratio) * (comp_index // NDIR).astype(jnp.float32))
    ice_loss = lax.dynamic_slice_in_dim(jnp.repeat(ice_rate, NDIR), first_comp, comps_dev, 0)
    partial = jnp.stack([jnp.sum(density, axis=-1), jnp.sum(density * levels, axis=-1)])
    other = band_swap(partial)
    energy_sum = partial[0] + other[0]
    moment = partial[1] + other[1]
    return sources(
        density,
        energy_sum,
        moment,
        levels,
        heading,
        ice_loss,
        sea_share,
        ice_share,
        wind_speed,
        wind_dir,
    )


def solution(mesh):
    return jax.shard_map(
        per_device,
        mesh=mesh,
        in_specs=(
            P("lat", "lon", "band"),
            P("lat", "lon"),
            P("lat", "lon"),
            P("lat", "lon"),
            P(),
            P(),
            P(None, "lat", "lon"),
            P("lat", "lon"),
            P("lat", "lon"),
            P(),
        ),
        out_specs=P("lat", "lon", "band"),
        check_vma=False,
    )
```

```python
import functools
import math

import jax
import jax.numpy as jnp
from jax import lax
from jax.experimental import pallas as pl
from jax.experimental.pallas import tpu as pltpu
from jax.sharding import PartitionSpec as P

NDIR = 36
ITERS = 4
NCOMP = 576


freq_ratio = 1.1
wind_gain = 0.12
break_coef = 0.05
south_edge = -30.0
band_span = 60.0


def quickest(behind, center, forward, beyond, courant):
    curvature = jnp.where(
        courant >= 0.0, forward - 2.0 * center + behind, beyond - 2.0 * forward + center
    )
    face_value = (
        0.5 * (center + forward)
        - 0.5 * courant * (forward - center)
        - (1.0 - courant * courant) / 6.0 * curvature
    )
    return courant * face_value


def advect(density, cell_speed, axis_dim):
    length = density.shape[axis_dim]

    def piece(array, low, high):
        return lax.slice_in_dim(array, low, high, axis=axis_dim)

    courant = 0.5 * (piece(cell_speed, 1, length - 2) + piece(cell_speed, 2, length - 1))
    fluxes = quickest(
        piece(density, 0, length - 3),
        piece(density, 1, length - 2),
        piece(density, 2, length - 1),
        piece(density, 3, length),
        courant,
    )
    faces = fluxes.shape[axis_dim]
    return piece(density, 2, length - 2) - (piece(fluxes, 1, faces) - piece(fluxes, 0, faces - 1))


def rotate(density, offset):
    dir_index = jnp.arange(density.shape[-1]) % NDIR
    target = dir_index + offset
    inner_roll = jnp.roll(density, -offset, axis=-1)
    if offset > 0:
        outer_roll = jnp.roll(density, NDIR - offset, axis=-1)
        return jnp.where(target >= NDIR, outer_roll, inner_roll)
    outer_roll = jnp.roll(density, -(offset + NDIR), axis=-1)
    return jnp.where(target < 0, outer_roll, inner_roll)


def refract(density, courant):
    fluxes = quickest(rotate(density, -1), density, rotate(density, 1), rotate(density, 2), courant)
    return density - (fluxes - rotate(fluxes, -1))


def expand(per_freq, spread):
    return jnp.dot(per_freq, spread, precision=lax.Precision.HIGHEST)


def lookup(classes, lookup_table):
    onehot = (classes[..., None] == jnp.arange(lookup_table.shape[0])).astype(jnp.float32)
    return jnp.dot(onehot, lookup_table, precision=lax.Precision.HIGHEST)


def stretch(rows, total_rows):
    latitude = (south_edge + band_span * (rows.astype(jnp.float32) + 0.5) / total_rows) * (
        math.pi / 180.0
    )
    return 1.0 / jnp.cos(latitude)


def sources(
    density,
    energy_sum,
    moment,
    levels,
    heading,
    ice_loss,
    sea_share,
    ice_share,
    wind_speed,
    wind_dir,
):
    mean_level = jnp.maximum(moment, 1.0) / jnp.maximum(energy_sum, 1.0)
    energy = energy_sum / NCOMP
    breaking = break_coef * levels * levels / mean_level[..., None] * (energy * energy)[..., None]
    growth = (
        wind_gain
        * wind_speed[..., None]
        * levels
        * jnp.maximum(jnp.cos(heading - wind_dir[..., None]), 0.0)
    )
    damping = ice_share[..., None] * ice_loss
    return sea_share[..., None] * density * jnp.exp(growth - breaking - damping)


INTERPRET = False
MESH_ID = pl.DeviceIdType.MESH
OFFSETS = [(a, b) for a in (-1, 0, 1) for b in (-1, 0, 1) if (a, b) != (0, 0)]


def halo_kernel(in_ref, out_ref, send_sem, recv_sem, *, halo):
    lon = lax.axis_index("lon")
    lat = lax.axis_index("lat")
    nlon = lax.axis_size("lon")
    nlat = lax.axis_size("lat")
    rows, cols = in_ref.shape[:2]

    def target(a, b):
        return {"lon": lax.rem(lon + b + nlon, nlon), "lat": lat + a}

    def has(a):
        return jnp.logical_and(lat + a >= 0, lat + a < nlat)

    def span(a, size):
        if a == 1:
            return pl.ds(size - halo, halo), pl.ds(0, halo)
        if a == -1:
            return pl.ds(0, halo), pl.ds(size + halo, halo)
        return pl.ds(0, size), pl.ds(halo, size)

    barrier = pltpu.get_barrier_semaphore()
    for a, b in OFFSETS:

        @pl.when(has(a))
        def _():
            pl.semaphore_signal(barrier, inc=1, device_id=target(a, b), device_id_type=MESH_ID)

    below = (lat + nlat - 1) // nlat
    above = 1 - lat // (nlat - 1)
    pl.semaphore_wait(barrier, 3 * (1 + below + above) - 1)

    copies = []
    for k, (a, b) in enumerate(OFFSETS):
        rows_src, rows_dst = span(a, rows)
        cols_src, cols_dst = span(b, cols)
        copy = pltpu.make_async_remote_copy(
            src_ref=in_ref.at[rows_src, cols_src],
            dst_ref=out_ref.at[rows_dst, cols_dst],
            send_sem=send_sem.at[k],
            recv_sem=recv_sem.at[k],
            device_id=target(a, b),
            device_id_type=MESH_ID,
        )
        pl.when(has(a))(copy.start)
        copies.append((a, copy))

    out_ref[pl.ds(halo, rows), pl.ds(halo, cols)] = in_ref[...]
    ghost = jnp.zeros((halo,) + out_ref.shape[1:], out_ref.dtype)

    @pl.when(lat == 0)
    def _():
        out_ref[pl.ds(0, halo)] = ghost

    @pl.when(lat == nlat - 1)
    def _():
        out_ref[pl.ds(rows + halo, halo)] = ghost

    for a, copy in copies:
        pl.when(has(a))(copy.wait_send)
        pl.when(has(-a))(copy.wait_recv)


def halo_exchange(cells, halo):
    rows, cols, chans = cells.shape
    vmem = pl.BlockSpec(memory_space=pltpu.VMEM)
    return pl.pallas_call(
        functools.partial(halo_kernel, halo=halo),
        out_shape=jax.ShapeDtypeStruct((rows + 2 * halo, cols + 2 * halo, chans), cells.dtype),
        in_specs=[vmem],
        out_specs=vmem,
        scratch_shapes=[pltpu.SemaphoreType.DMA((8,)), pltpu.SemaphoreType.DMA((8,))],
        compiler_params=pltpu.CompilerParams(collective_id=0, has_side_effects=True),
        interpret=pltpu.InterpretParams(detect_races=True) if INTERPRET else False,
    )(cells)


def exchange(cells, axis, dim, width, closed):
    count = lax.axis_size(axis)
    ends = count if closed else count - 1
    head = lax.slice_in_dim(cells, 0, width, axis=dim)
    tail = lax.slice_in_dim(cells, cells.shape[dim] - width, cells.shape[dim], axis=dim)
    before = lax.ppermute(tail, axis, [(i, (i + 1) % count) for i in range(ends)])
    after = lax.ppermute(head, axis, [((i + 1) % count, i) for i in range(ends)])
    return jnp.concatenate([before, cells, after], axis=dim)


def trim(array, dim, amount):
    return lax.slice_in_dim(array, amount, array.shape[dim] - amount, axis=dim)


def per_device(
    spectrum,
    sea_mask,
    ice_mask,
    depth_class,
    speed_table,
    refraction_table,
    depth_slope,
    wind_speed,
    wind_dir,
    ice_rate,
):
    rows_dev, cols_dev, comps_dev = spectrum.shape
    freqs_dev = comps_dev // NDIR
    halo = 2 * ITERS
    band_index = lax.axis_index("band")
    first_comp = band_index * comps_dev
    local_comp = jnp.arange(comps_dev)
    comp_index = first_comp + local_comp
    spread = (local_comp[None, :] // NDIR == jnp.arange(freqs_dev)[:, None]).astype(jnp.float32)
    heading = 2.0 * math.pi * (comp_index % NDIR).astype(jnp.float32) / NDIR
    face_angle = heading + math.pi / NDIR
    cos_head = jnp.cos(heading)
    sin_head = jnp.sin(heading)
    sin_face = jnp.sin(face_angle)
    cos_face = jnp.cos(face_angle)
    sea_share = sea_mask.astype(jnp.float32)
    ice_share = ice_mask.astype(jnp.float32)
    speed_local = lax.dynamic_slice_in_dim(speed_table, band_index * freqs_dev, freqs_dev, 1)
    refr_local = lax.dynamic_slice_in_dim(refraction_table, band_index * freqs_dev, freqs_dev, 1)
    point_inputs = [sea_share, depth_class.astype(jnp.float32), depth_slope[0], depth_slope[1]]
    stacked = jnp.concatenate([spectrum] + [v[..., None] for v in point_inputs], axis=-1)
    stacked = halo_exchange(stacked, halo)
    sea_ext, class_ext, slope_x, slope_y = [stacked[..., comps_dev + i] for i in range(4)]
    classes = jnp.arange(speed_table.shape[0]).astype(jnp.float32)
    chosen = (class_ext[..., None] == classes)[..., None]
    group_speed = jnp.sum(jnp.where(chosen, speed_local, 0.0), axis=2) * sea_ext[..., None]
    turning = jnp.sum(jnp.where(chosen, refr_local, 0.0), axis=2) * sea_ext[..., None]
    turn_x = turning * slope_x[..., None]
    turn_y = turning * slope_y[..., None]
    density = stacked[..., :comps_dev] * sea_ext[..., None]
    fields = jnp.concatenate([group_speed, turn_x, turn_y], axis=-1)

    total_rows = rows_dev * lax.axis_size("lat")
    first_row = lax.axis_index("lat") * rows_dev - halo
    rows_ext = first_row + jnp.arange(rows_dev + 2 * halo)
    inside = ((rows_ext >= 0) & (rows_ext < total_rows))[:, None, None]
    stretch_rows = stretch(rows_ext, total_rows)
    gs_ext = expand(fields[..., :freqs_dev], spread)
    along_x = gs_ext * cos_head * stretch_rows[:, None, None]
    along_y = gs_ext * sin_head
    along_t = (
        expand(fields[..., freqs_dev : 2 * freqs_dev], spread) * sin_face
        - expand(fields[..., 2 * freqs_dev :], spread) * cos_face
    )
    for substep in range(ITERS):
        density = advect(density, along_x, 1)
        along_x, along_y, along_t = [trim(a, 1, 2) for a in (along_x, along_y, along_t)]
        density = advect(density, along_y, 0)
        inside = trim(inside, 0, 2)
        density = jnp.where(inside, density, 0.0)
        along_x, along_y, along_t = [trim(a, 0, 2) for a in (along_x, along_y, along_t)]
        density = refract(density, along_t)

    levels = jnp.exp(math.log(freq_ratio) * (comp_index // NDIR).astype(jnp.float32))
    ice_loss = lax.dynamic_slice_in_dim(jnp.repeat(ice_rate, NDIR), first_comp, comps_dev, 0)
    partial = jnp.stack([jnp.sum(density, axis=-1), jnp.sum(density * levels, axis=-1)])
    other = lax.ppermute(partial, "band", [(0, 1), (1, 0)])
    energy_sum = partial[0] + other[0]
    moment = partial[1] + other[1]
    return sources(
        density,
        energy_sum,
        moment,
        levels,
        heading,
        ice_loss,
        sea_share,
        ice_share,
        wind_speed,
        wind_dir,
    )


def solution(mesh):
    return jax.shard_map(
        per_device,
        mesh=mesh,
        in_specs=(
            P("lat", "lon", "band"),
            P("lat", "lon"),
            P("lat", "lon"),
            P("lat", "lon"),
            P(),
            P(),
            P(None, "lat", "lon"),
            P("lat", "lon"),
            P("lat", "lon"),
            P(),
        ),
        out_specs=P("lat", "lon", "band"),
        check_vma=False,
    )
```

```python
import functools
import math

import jax
import jax.numpy as jnp
from jax import lax
from jax.experimental import pallas as pl
from jax.experimental.pallas import tpu as pltpu
from jax.sharding import PartitionSpec as P

NDIR = 36
ITERS = 4
NCOMP = 576


freq_ratio = 1.1
wind_gain = 0.12
break_coef = 0.05
south_edge = -30.0
band_span = 60.0


def quickest(behind, center, forward, beyond, courant):
    curvature = jnp.where(
        courant >= 0.0, forward - 2.0 * center + behind, beyond - 2.0 * forward + center
    )
    face_value = (
        0.5 * (center + forward)
        - 0.5 * courant * (forward - center)
        - (1.0 - courant * courant) / 6.0 * curvature
    )
    return courant * face_value


def advect(density, cell_speed, axis_dim):
    length = density.shape[axis_dim]

    def piece(array, low, high):
        return lax.slice_in_dim(array, low, high, axis=axis_dim)

    courant = 0.5 * (piece(cell_speed, 1, length - 2) + piece(cell_speed, 2, length - 1))
    fluxes = quickest(
        piece(density, 0, length - 3),
        piece(density, 1, length - 2),
        piece(density, 2, length - 1),
        piece(density, 3, length),
        courant,
    )
    faces = fluxes.shape[axis_dim]
    return piece(density, 2, length - 2) - (piece(fluxes, 1, faces) - piece(fluxes, 0, faces - 1))


def shifted(density, offset):
    edges = [(0, 0, 0)] * (density.ndim - 1) + [(-offset, offset, 0)]
    return lax.pad(density, jnp.zeros((), density.dtype), edges)


def rotate(density, offset):
    dir_index = jnp.arange(density.shape[-1]) % NDIR
    target = dir_index + offset
    inner = shifted(density, offset)
    if offset > 0:
        return jnp.where(target >= NDIR, shifted(density, offset - NDIR), inner)
    return jnp.where(target < 0, shifted(density, offset + NDIR), inner)


def refract(density, courant):
    fluxes = quickest(rotate(density, -1), density, rotate(density, 1), rotate(density, 2), courant)
    return density - (fluxes - rotate(fluxes, -1))


def expand(per_freq, spread):
    return jnp.dot(per_freq, spread, precision=lax.Precision.HIGHEST)


def lookup(classes, lookup_table):
    onehot = (classes[..., None] == jnp.arange(lookup_table.shape[0])).astype(jnp.float32)
    return jnp.dot(onehot, lookup_table, precision=lax.Precision.HIGHEST)


def stretch(rows, total_rows):
    latitude = (south_edge + band_span * (rows.astype(jnp.float32) + 0.5) / total_rows) * (
        math.pi / 180.0
    )
    return 1.0 / jnp.cos(latitude)


def sources(
    density,
    energy_sum,
    moment,
    levels,
    heading,
    ice_loss,
    sea_share,
    ice_share,
    wind_speed,
    wind_dir,
):
    mean_level = jnp.maximum(moment, 1.0) / jnp.maximum(energy_sum, 1.0)
    energy = energy_sum / NCOMP
    breaking = break_coef * levels * levels / mean_level[..., None] * (energy * energy)[..., None]
    growth = (
        wind_gain
        * wind_speed[..., None]
        * levels
        * jnp.maximum(jnp.cos(heading - wind_dir[..., None]), 0.0)
    )
    damping = ice_share[..., None] * ice_loss
    return sea_share[..., None] * density * jnp.exp(growth - breaking - damping)


INTERPRET = False
MESH_ID = pl.DeviceIdType.MESH
OFFSETS = [(a, b) for a in (-1, 0, 1) for b in (-1, 0, 1) if (a, b) != (0, 0)]


def halo_kernel(in_ref, out_ref, send_sem, recv_sem, *, halo):
    lon = lax.axis_index("lon")
    lat = lax.axis_index("lat")
    nlon = lax.axis_size("lon")
    nlat = lax.axis_size("lat")
    rows, cols = in_ref.shape[:2]

    def target(a, b):
        return {"lon": lax.rem(lon + b + nlon, nlon), "lat": lat + a}

    def has(a):
        return jnp.logical_and(lat + a >= 0, lat + a < nlat)

    def span(a, size):
        if a == 1:
            return pl.ds(size - halo, halo), pl.ds(0, halo)
        if a == -1:
            return pl.ds(0, halo), pl.ds(size + halo, halo)
        return pl.ds(0, size), pl.ds(halo, size)

    barrier = pltpu.get_barrier_semaphore()
    for a, b in OFFSETS:

        @pl.when(has(a))
        def _():
            pl.semaphore_signal(barrier, inc=1, device_id=target(a, b), device_id_type=MESH_ID)

    below = (lat + nlat - 1) // nlat
    above = 1 - lat // (nlat - 1)
    pl.semaphore_wait(barrier, 3 * (1 + below + above) - 1)

    copies = []
    for k, (a, b) in enumerate(OFFSETS):
        rows_src, rows_dst = span(a, rows)
        cols_src, cols_dst = span(b, cols)
        copy = pltpu.make_async_remote_copy(
            src_ref=in_ref.at[rows_src, cols_src],
            dst_ref=out_ref.at[rows_dst, cols_dst],
            send_sem=send_sem.at[k],
            recv_sem=recv_sem.at[k],
            device_id=target(a, b),
            device_id_type=MESH_ID,
        )
        pl.when(has(a))(copy.start)
        copies.append((a, copy))

    out_ref[pl.ds(halo, rows), pl.ds(halo, cols)] = in_ref[...]
    ghost = jnp.zeros((halo,) + out_ref.shape[1:], out_ref.dtype)

    @pl.when(lat == 0)
    def _():
        out_ref[pl.ds(0, halo)] = ghost

    @pl.when(lat == nlat - 1)
    def _():
        out_ref[pl.ds(rows + halo, halo)] = ghost

    for a, copy in copies:
        pl.when(has(a))(copy.wait_send)
        pl.when(has(-a))(copy.wait_recv)


def halo_exchange(cells, halo):
    rows, cols, chans = cells.shape
    vmem = pl.BlockSpec(memory_space=pltpu.VMEM)
    return pl.pallas_call(
        functools.partial(halo_kernel, halo=halo),
        out_shape=jax.ShapeDtypeStruct((rows + 2 * halo, cols + 2 * halo, chans), cells.dtype),
        in_specs=[vmem],
        out_specs=vmem,
        scratch_shapes=[pltpu.SemaphoreType.DMA((8,)), pltpu.SemaphoreType.DMA((8,))],
        compiler_params=pltpu.CompilerParams(collective_id=0, has_side_effects=True),
        interpret=pltpu.InterpretParams(detect_races=True) if INTERPRET else False,
    )(cells)


def exchange(cells, axis, dim, width, closed):
    count = lax.axis_size(axis)
    ends = count if closed else count - 1
    head = lax.slice_in_dim(cells, 0, width, axis=dim)
    tail = lax.slice_in_dim(cells, cells.shape[dim] - width, cells.shape[dim], axis=dim)
    before = lax.ppermute(tail, axis, [(i, (i + 1) % count) for i in range(ends)])
    after = lax.ppermute(head, axis, [((i + 1) % count, i) for i in range(ends)])
    return jnp.concatenate([before, cells, after], axis=dim)


def trim(array, dim, amount):
    return lax.slice_in_dim(array, amount, array.shape[dim] - amount, axis=dim)


def per_device(
    spectrum,
    sea_mask,
    ice_mask,
    depth_class,
    speed_table,
    refraction_table,
    depth_slope,
    wind_speed,
    wind_dir,
    ice_rate,
):
    rows_dev, cols_dev, comps_dev = spectrum.shape
    freqs_dev = comps_dev // NDIR
    halo = 2 * ITERS
    band_index = lax.axis_index("band")
    first_comp = band_index * comps_dev
    local_comp = jnp.arange(comps_dev)
    comp_index = first_comp + local_comp
    spread = (local_comp[None, :] // NDIR == jnp.arange(freqs_dev)[:, None]).astype(jnp.float32)
    heading = 2.0 * math.pi * (comp_index % NDIR).astype(jnp.float32) / NDIR
    face_angle = heading + math.pi / NDIR
    cos_head = jnp.cos(heading)
    sin_head = jnp.sin(heading)
    sin_face = jnp.sin(face_angle)
    cos_face = jnp.cos(face_angle)
    sea_share = sea_mask.astype(jnp.float32)
    ice_share = ice_mask.astype(jnp.float32)
    speed_local = lax.dynamic_slice_in_dim(speed_table, band_index * freqs_dev, freqs_dev, 1)
    refr_local = lax.dynamic_slice_in_dim(refraction_table, band_index * freqs_dev, freqs_dev, 1)
    chosen = (depth_class[..., None] == jnp.arange(speed_table.shape[0]))[..., None]
    group_speed = jnp.sum(jnp.where(chosen, speed_local, 0.0), axis=2) * sea_share[..., None]
    turning = jnp.sum(jnp.where(chosen, refr_local, 0.0), axis=2) * sea_share[..., None]
    turn_x = turning * depth_slope[0][..., None]
    turn_y = turning * depth_slope[1][..., None]
    density = spectrum * sea_share[..., None]

    stacked = jnp.concatenate([density, group_speed, turn_x, turn_y], axis=-1)
    stacked = halo_exchange(stacked, halo)
    density = stacked[..., :comps_dev]
    fields = stacked[..., comps_dev:]

    total_rows = rows_dev * lax.axis_size("lat")
    first_row = lax.axis_index("lat") * rows_dev - halo
    rows_ext = first_row + jnp.arange(rows_dev + 2 * halo)
    inside = ((rows_ext >= 0) & (rows_ext < total_rows))[:, None, None]
    stretch_rows = stretch(rows_ext, total_rows)
    gs_ext = expand(fields[..., :freqs_dev], spread)
    along_x = gs_ext * cos_head * stretch_rows[:, None, None]
    along_y = gs_ext * sin_head
    along_t = (
        expand(fields[..., freqs_dev : 2 * freqs_dev], spread) * sin_face
        - expand(fields[..., 2 * freqs_dev :], spread) * cos_face
    )
    for substep in range(ITERS):
        density = advect(density, along_x, 1)
        along_x, along_y, along_t = [trim(a, 1, 2) for a in (along_x, along_y, along_t)]
        density = advect(density, along_y, 0)
        inside = trim(inside, 0, 2)
        density = jnp.where(inside, density, 0.0)
        along_x, along_y, along_t = [trim(a, 0, 2) for a in (along_x, along_y, along_t)]
        density = refract(density, along_t)

    levels = jnp.exp(math.log(freq_ratio) * (comp_index // NDIR).astype(jnp.float32))
    ice_loss = lax.dynamic_slice_in_dim(jnp.repeat(ice_rate, NDIR), first_comp, comps_dev, 0)
    partial = jnp.stack([jnp.sum(density, axis=-1), jnp.sum(density * levels, axis=-1)])
    other = lax.ppermute(partial, "band", [(0, 1), (1, 0)])
    energy_sum = partial[0] + other[0]
    moment = partial[1] + other[1]
    return sources(
        density,
        energy_sum,
        moment,
        levels,
        heading,
        ice_loss,
        sea_share,
        ice_share,
        wind_speed,
        wind_dir,
    )


def solution(mesh):
    return jax.shard_map(
        per_device,
        mesh=mesh,
        in_specs=(
            P("lat", "lon", "band"),
            P("lat", "lon"),
            P("lat", "lon"),
            P("lat", "lon"),
            P(),
            P(),
            P(None, "lat", "lon"),
            P("lat", "lon"),
            P("lat", "lon"),
            P(),
        ),
        out_specs=P("lat", "lon", "band"),
        check_vma=False,
    )
```

```python
import functools
import math

import jax
import jax.numpy as jnp
from jax import lax
from jax.experimental import pallas as pl
from jax.experimental.pallas import tpu as pltpu
from jax.sharding import PartitionSpec as P

NDIR = 36
ITERS = 4
NCOMP = 576


freq_ratio = 1.1
wind_gain = 0.12
break_coef = 0.05
south_edge = -30.0
band_span = 60.0


def quickest(behind, center, forward, beyond, courant):
    curvature = jnp.where(
        courant >= 0.0, forward - 2.0 * center + behind, beyond - 2.0 * forward + center
    )
    face_value = (
        0.5 * (center + forward)
        - 0.5 * courant * (forward - center)
        - (1.0 - courant * courant) / 6.0 * curvature
    )
    return courant * face_value


def advect(density, cell_speed, axis_dim):
    length = density.shape[axis_dim]

    def piece(array, low):
        return lax.slice_in_dim(array, low, low + length - 4, axis=axis_dim)

    def face(low):
        courant = 0.5 * (piece(cell_speed, low + 1) + piece(cell_speed, low + 2))
        return quickest(*[piece(density, low + i) for i in range(4)], courant)

    return piece(density, 2) - (face(1) - face(0))


def shifted(density, offset):
    edges = [(0, 0, 0)] * (density.ndim - 1) + [(-offset, offset, 0)]
    return lax.pad(density, jnp.zeros((), density.dtype), edges)


def rotate(density, offset):
    dir_index = jnp.arange(density.shape[-1]) % NDIR
    target = dir_index + offset
    inner = shifted(density, offset)
    if offset > 0:
        return jnp.where(target >= NDIR, shifted(density, offset - NDIR), inner)
    return jnp.where(target < 0, shifted(density, offset + NDIR), inner)


def refract(density, courant, courant_behind):
    behind = rotate(density, -1)
    forward = rotate(density, 1)
    fluxes = quickest(behind, density, forward, rotate(density, 2), courant)
    behind_fluxes = quickest(rotate(density, -2), behind, density, forward, courant_behind)
    return density - (fluxes - behind_fluxes)


def expand(per_freq, spread):
    return jnp.dot(per_freq, spread, precision=lax.Precision.HIGHEST)


def lookup(classes, lookup_table):
    onehot = (classes[..., None] == jnp.arange(lookup_table.shape[0])).astype(jnp.float32)
    return jnp.dot(onehot, lookup_table, precision=lax.Precision.HIGHEST)


def stretch(rows, total_rows):
    latitude = (south_edge + band_span * (rows.astype(jnp.float32) + 0.5) / total_rows) * (
        math.pi / 180.0
    )
    return 1.0 / jnp.cos(latitude)


def sources(
    density,
    energy_sum,
    moment,
    levels,
    heading,
    ice_loss,
    sea_share,
    ice_share,
    wind_speed,
    wind_dir,
):
    mean_level = jnp.maximum(moment, 1.0) / jnp.maximum(energy_sum, 1.0)
    energy = energy_sum / NCOMP
    breaking = break_coef * levels * levels / mean_level[..., None] * (energy * energy)[..., None]
    growth = (
        wind_gain
        * wind_speed[..., None]
        * levels
        * jnp.maximum(jnp.cos(heading - wind_dir[..., None]), 0.0)
    )
    damping = ice_share[..., None] * ice_loss
    return sea_share[..., None] * density * jnp.exp(growth - breaking - damping)


INTERPRET = False
MESH_ID = pl.DeviceIdType.MESH
OFFSETS = [(a, b) for a in (-1, 0, 1) for b in (-1, 0, 1) if (a, b) != (0, 0)]


def halo_kernel(in_ref, out_ref, send_sem, recv_sem, *, halo):
    lon = lax.axis_index("lon")
    lat = lax.axis_index("lat")
    nlon = lax.axis_size("lon")
    nlat = lax.axis_size("lat")
    rows, cols = in_ref.shape[:2]

    def target(a, b):
        return {"lon": lax.rem(lon + b + nlon, nlon), "lat": lat + a}

    def has(a):
        return jnp.logical_and(lat + a >= 0, lat + a < nlat)

    def span(a, size):
        if a == 1:
            return pl.ds(size - halo, halo), pl.ds(0, halo)
        if a == -1:
            return pl.ds(0, halo), pl.ds(size + halo, halo)
        return pl.ds(0, size), pl.ds(halo, size)

    barrier = pltpu.get_barrier_semaphore()
    for a, b in OFFSETS:

        @pl.when(has(a))
        def _():
            pl.semaphore_signal(barrier, inc=1, device_id=target(a, b), device_id_type=MESH_ID)

    below = (lat + nlat - 1) // nlat
    above = 1 - lat // (nlat - 1)
    pl.semaphore_wait(barrier, 3 * (1 + below + above) - 1)

    copies = []
    for k, (a, b) in enumerate(OFFSETS):
        rows_src, rows_dst = span(a, rows)
        cols_src, cols_dst = span(b, cols)
        copy = pltpu.make_async_remote_copy(
            src_ref=in_ref.at[rows_src, cols_src],
            dst_ref=out_ref.at[rows_dst, cols_dst],
            send_sem=send_sem.at[k],
            recv_sem=recv_sem.at[k],
            device_id=target(a, b),
            device_id_type=MESH_ID,
        )
        pl.when(has(a))(copy.start)
        copies.append((a, copy))

    out_ref[pl.ds(halo, rows), pl.ds(halo, cols)] = in_ref[...]
    ghost = jnp.zeros((halo,) + out_ref.shape[1:], out_ref.dtype)

    @pl.when(lat == 0)
    def _():
        out_ref[pl.ds(0, halo)] = ghost

    @pl.when(lat == nlat - 1)
    def _():
        out_ref[pl.ds(rows + halo, halo)] = ghost

    for a, copy in copies:
        pl.when(has(a))(copy.wait_send)
        pl.when(has(-a))(copy.wait_recv)


def halo_exchange(cells, halo):
    rows, cols, chans = cells.shape
    vmem = pl.BlockSpec(memory_space=pltpu.VMEM)
    return pl.pallas_call(
        functools.partial(halo_kernel, halo=halo),
        out_shape=jax.ShapeDtypeStruct((rows + 2 * halo, cols + 2 * halo, chans), cells.dtype),
        in_specs=[vmem],
        out_specs=vmem,
        scratch_shapes=[pltpu.SemaphoreType.DMA((8,)), pltpu.SemaphoreType.DMA((8,))],
        compiler_params=pltpu.CompilerParams(collective_id=0, has_side_effects=True),
        interpret=pltpu.InterpretParams(detect_races=True) if INTERPRET else False,
    )(cells)


def exchange(cells, axis, dim, width, closed):
    count = lax.axis_size(axis)
    ends = count if closed else count - 1
    head = lax.slice_in_dim(cells, 0, width, axis=dim)
    tail = lax.slice_in_dim(cells, cells.shape[dim] - width, cells.shape[dim], axis=dim)
    before = lax.ppermute(tail, axis, [(i, (i + 1) % count) for i in range(ends)])
    after = lax.ppermute(head, axis, [((i + 1) % count, i) for i in range(ends)])
    return jnp.concatenate([before, cells, after], axis=dim)


def trim(array, dim, amount):
    return lax.slice_in_dim(array, amount, array.shape[dim] - amount, axis=dim)


def per_device(
    spectrum,
    sea_mask,
    ice_mask,
    depth_class,
    speed_table,
    refraction_table,
    depth_slope,
    wind_speed,
    wind_dir,
    ice_rate,
):
    rows_dev, cols_dev, comps_dev = spectrum.shape
    freqs_dev = comps_dev // NDIR
    halo = 2 * ITERS
    band_index = lax.axis_index("band")
    first_comp = band_index * comps_dev
    local_comp = jnp.arange(comps_dev)
    comp_index = first_comp + local_comp
    spread = (local_comp[None, :] // NDIR == jnp.arange(freqs_dev)[:, None]).astype(jnp.float32)
    heading = 2.0 * math.pi * (comp_index % NDIR).astype(jnp.float32) / NDIR
    face_angle = heading + math.pi / NDIR
    cos_head = jnp.cos(heading)
    sin_head = jnp.sin(heading)
    sin_face = jnp.sin(face_angle)
    cos_face = jnp.cos(face_angle)
    sea_share = sea_mask.astype(jnp.float32)
    ice_share = ice_mask.astype(jnp.float32)
    speed_local = lax.dynamic_slice_in_dim(speed_table, band_index * freqs_dev, freqs_dev, 1)
    refr_local = lax.dynamic_slice_in_dim(refraction_table, band_index * freqs_dev, freqs_dev, 1)
    chosen = (depth_class[..., None] == jnp.arange(speed_table.shape[0]))[..., None]
    group_speed = jnp.sum(jnp.where(chosen, speed_local, 0.0), axis=2) * sea_share[..., None]
    turning = jnp.sum(jnp.where(chosen, refr_local, 0.0), axis=2) * sea_share[..., None]
    turn_x = turning * depth_slope[0][..., None]
    turn_y = turning * depth_slope[1][..., None]
    density = spectrum * sea_share[..., None]

    stacked = jnp.concatenate([density, group_speed, turn_x, turn_y], axis=-1)
    stacked = halo_exchange(stacked, halo)
    density = stacked[..., :comps_dev]
    fields = stacked[..., comps_dev:]

    total_rows = rows_dev * lax.axis_size("lat")
    first_row = lax.axis_index("lat") * rows_dev - halo
    rows_ext = first_row + jnp.arange(rows_dev + 2 * halo)
    inside = ((rows_ext >= 0) & (rows_ext < total_rows))[:, None, None]
    stretch_rows = stretch(rows_ext, total_rows)
    gs_ext = expand(fields[..., :freqs_dev], spread)
    along_x = gs_ext * cos_head * stretch_rows[:, None, None]
    along_y = gs_ext * sin_head
    along_t = (
        expand(fields[..., freqs_dev : 2 * freqs_dev], spread) * sin_face
        - expand(fields[..., 2 * freqs_dev :], spread) * cos_face
    )
    along_t_behind = rotate(along_t, -1)
    for substep in range(ITERS):
        density = advect(density, along_x, 1)
        along_x, along_y, along_t, along_t_behind = [
            trim(a, 1, 2) for a in (along_x, along_y, along_t, along_t_behind)
        ]
        density = advect(density, along_y, 0)
        inside = trim(inside, 0, 2)
        density = jnp.where(inside, density, 0.0)
        along_x, along_y, along_t, along_t_behind = [
            trim(a, 0, 2) for a in (along_x, along_y, along_t, along_t_behind)
        ]
        density = refract(density, along_t, along_t_behind)

    levels = jnp.exp(math.log(freq_ratio) * (comp_index // NDIR).astype(jnp.float32))
    ice_loss = lax.dynamic_slice_in_dim(jnp.repeat(ice_rate, NDIR), first_comp, comps_dev, 0)
    partial = jnp.stack([jnp.sum(density, axis=-1), jnp.sum(density * levels, axis=-1)])
    other = lax.ppermute(partial, "band", [(0, 1), (1, 0)])
    energy_sum = partial[0] + other[0]
    moment = partial[1] + other[1]
    return sources(
        density,
        energy_sum,
        moment,
        levels,
        heading,
        ice_loss,
        sea_share,
        ice_share,
        wind_speed,
        wind_dir,
    )


def solution(mesh):
    return jax.shard_map(
        per_device,
        mesh=mesh,
        in_specs=(
            P("lat", "lon", "band"),
            P("lat", "lon"),
            P("lat", "lon"),
            P("lat", "lon"),
            P(),
            P(),
            P(None, "lat", "lon"),
            P("lat", "lon"),
            P("lat", "lon"),
            P(),
        ),
        out_specs=P("lat", "lon", "band"),
        check_vma=False,
    )
```

```python
import functools
import math

import jax
import jax.numpy as jnp
from jax import lax
from jax.experimental import pallas as pl
from jax.experimental.pallas import tpu as pltpu
from jax.sharding import PartitionSpec as P

NDIR = 36
ITERS = 4
NCOMP = 576


freq_ratio = 1.1
wind_gain = 0.12
break_coef = 0.05
south_edge = -30.0
band_span = 60.0


def quickest(behind, center, forward, beyond, courant):
    curvature = jnp.where(
        courant >= 0.0, forward - 2.0 * center + behind, beyond - 2.0 * forward + center
    )
    face_value = (
        0.5 * (center + forward)
        - 0.5 * courant * (forward - center)
        - (1.0 - courant * courant) / 6.0 * curvature
    )
    return courant * face_value


def advect(density, cell_speed, axis_dim):
    length = density.shape[axis_dim]

    def piece(array, low):
        return lax.slice_in_dim(array, low, low + length - 4, axis=axis_dim)

    def face(low):
        courant = 0.5 * (piece(cell_speed, low + 1) + piece(cell_speed, low + 2))
        return quickest(*[piece(density, low + i) for i in range(4)], courant)

    return piece(density, 2) - (face(1) - face(0))


def shifted(density, offset):
    edges = [(0, 0, 0)] * (density.ndim - 1) + [(-offset, offset, 0)]
    return lax.pad(density, jnp.zeros((), density.dtype), edges)


def rotate(density, offset):
    dir_index = jnp.arange(density.shape[-1]) % NDIR
    target = dir_index + offset
    inner = shifted(density, offset)
    if offset > 0:
        return jnp.where(target >= NDIR, shifted(density, offset - NDIR), inner)
    return jnp.where(target < 0, shifted(density, offset + NDIR), inner)


def refract(density, courant):
    fluxes = quickest(rotate(density, -1), density, rotate(density, 1), rotate(density, 2), courant)
    return density - (fluxes - rotate(fluxes, -1))


def expand(per_freq, spread):
    return jnp.dot(per_freq, spread, precision=lax.Precision.HIGHEST)


def lookup(classes, lookup_table):
    onehot = (classes[..., None] == jnp.arange(lookup_table.shape[0])).astype(jnp.float32)
    return jnp.dot(onehot, lookup_table, precision=lax.Precision.HIGHEST)


def stretch(rows, total_rows):
    latitude = (south_edge + band_span * (rows.astype(jnp.float32) + 0.5) / total_rows) * (
        math.pi / 180.0
    )
    return 1.0 / jnp.cos(latitude)


def sources(
    density,
    energy_sum,
    moment,
    levels,
    heading,
    ice_loss,
    sea_share,
    ice_share,
    wind_speed,
    wind_dir,
):
    mean_level = jnp.maximum(moment, 1.0) / jnp.maximum(energy_sum, 1.0)
    energy = energy_sum / NCOMP
    breaking = break_coef * levels * levels / mean_level[..., None] * (energy * energy)[..., None]
    growth = (
        wind_gain
        * wind_speed[..., None]
        * levels
        * jnp.maximum(jnp.cos(heading - wind_dir[..., None]), 0.0)
    )
    damping = ice_share[..., None] * ice_loss
    return sea_share[..., None] * density * jnp.exp(growth - breaking - damping)


INTERPRET = False
MESH_ID = pl.DeviceIdType.MESH
OFFSETS = [(a, b) for a in (-1, 0, 1) for b in (-1, 0, 1) if (a, b) != (0, 0)]


def halo_kernel(in_ref, out_ref, send_sem, recv_sem, *, halo):
    lon = lax.axis_index("lon")
    lat = lax.axis_index("lat")
    nlon = lax.axis_size("lon")
    nlat = lax.axis_size("lat")
    rows, cols = in_ref.shape[:2]

    def target(a, b):
        return {"lon": lax.rem(lon + b + nlon, nlon), "lat": lat + a}

    def has(a):
        return jnp.logical_and(lat + a >= 0, lat + a < nlat)

    def span(a, size):
        if a == 1:
            return pl.ds(size - halo, halo), pl.ds(0, halo)
        if a == -1:
            return pl.ds(0, halo), pl.ds(size + halo, halo)
        return pl.ds(0, size), pl.ds(halo, size)

    barrier = pltpu.get_barrier_semaphore()
    for a, b in OFFSETS:

        @pl.when(has(a))
        def _():
            pl.semaphore_signal(barrier, inc=1, device_id=target(a, b), device_id_type=MESH_ID)

    below = (lat + nlat - 1) // nlat
    above = 1 - lat // (nlat - 1)
    pl.semaphore_wait(barrier, 3 * (1 + below + above) - 1)

    copies = []
    for k, (a, b) in enumerate(OFFSETS):
        rows_src, rows_dst = span(a, rows)
        cols_src, cols_dst = span(b, cols)
        copy = pltpu.make_async_remote_copy(
            src_ref=in_ref.at[rows_src, cols_src],
            dst_ref=out_ref.at[rows_dst, cols_dst],
            send_sem=send_sem.at[k],
            recv_sem=recv_sem.at[k],
            device_id=target(a, b),
            device_id_type=MESH_ID,
        )
        pl.when(has(a))(copy.start)
        copies.append((a, copy))

    out_ref[pl.ds(halo, rows), pl.ds(halo, cols)] = in_ref[...]
    ghost = jnp.zeros((halo,) + out_ref.shape[1:], out_ref.dtype)

    @pl.when(lat == 0)
    def _():
        out_ref[pl.ds(0, halo)] = ghost

    @pl.when(lat == nlat - 1)
    def _():
        out_ref[pl.ds(rows + halo, halo)] = ghost

    for a, copy in copies:
        pl.when(has(a))(copy.wait_send)
        pl.when(has(-a))(copy.wait_recv)


def halo_exchange(cells, halo):
    rows, cols, chans = cells.shape
    vmem = pl.BlockSpec(memory_space=pltpu.VMEM)
    return pl.pallas_call(
        functools.partial(halo_kernel, halo=halo),
        out_shape=jax.ShapeDtypeStruct((rows + 2 * halo, cols + 2 * halo, chans), cells.dtype),
        in_specs=[vmem],
        out_specs=vmem,
        scratch_shapes=[pltpu.SemaphoreType.DMA((8,)), pltpu.SemaphoreType.DMA((8,))],
        compiler_params=pltpu.CompilerParams(collective_id=0, has_side_effects=True),
        interpret=pltpu.InterpretParams(detect_races=True) if INTERPRET else False,
    )(cells)


def exchange(cells, axis, dim, width, closed):
    count = lax.axis_size(axis)
    ends = count if closed else count - 1
    head = lax.slice_in_dim(cells, 0, width, axis=dim)
    tail = lax.slice_in_dim(cells, cells.shape[dim] - width, cells.shape[dim], axis=dim)
    before = lax.ppermute(tail, axis, [(i, (i + 1) % count) for i in range(ends)])
    after = lax.ppermute(head, axis, [((i + 1) % count, i) for i in range(ends)])
    return jnp.concatenate([before, cells, after], axis=dim)


def trim(array, dim, amount):
    return lax.slice_in_dim(array, amount, array.shape[dim] - amount, axis=dim)


def per_device(
    spectrum,
    sea_mask,
    ice_mask,
    depth_class,
    speed_table,
    refraction_table,
    depth_slope,
    wind_speed,
    wind_dir,
    ice_rate,
):
    rows_dev, cols_dev, comps_dev = spectrum.shape
    freqs_dev = comps_dev // NDIR
    halo = 2 * ITERS
    band_index = lax.axis_index("band")
    first_comp = band_index * comps_dev
    local_comp = jnp.arange(comps_dev)
    comp_index = first_comp + local_comp
    spread = (local_comp[None, :] // NDIR == jnp.arange(freqs_dev)[:, None]).astype(jnp.float32)
    heading = 2.0 * math.pi * (comp_index % NDIR).astype(jnp.float32) / NDIR
    face_angle = heading + math.pi / NDIR
    cos_head = jnp.cos(heading)
    sin_head = jnp.sin(heading)
    sin_face = jnp.sin(face_angle)
    cos_face = jnp.cos(face_angle)
    sea_share = sea_mask.astype(jnp.float32)
    ice_share = ice_mask.astype(jnp.float32)
    speed_local = lax.dynamic_slice_in_dim(speed_table, band_index * freqs_dev, freqs_dev, 1)
    refr_local = lax.dynamic_slice_in_dim(refraction_table, band_index * freqs_dev, freqs_dev, 1)
    chosen = (depth_class[..., None] == jnp.arange(speed_table.shape[0]))[..., None]
    group_speed = jnp.sum(jnp.where(chosen, speed_local, 0.0), axis=2) * sea_share[..., None]
    turning = jnp.sum(jnp.where(chosen, refr_local, 0.0), axis=2) * sea_share[..., None]
    turn_x = turning * depth_slope[0][..., None]
    turn_y = turning * depth_slope[1][..., None]
    density = spectrum * sea_share[..., None]

    stacked = jnp.concatenate([density, group_speed, turn_x, turn_y], axis=-1)
    stacked = halo_exchange(stacked, halo)
    density = stacked[..., :comps_dev]
    fields = stacked[..., comps_dev:]

    total_rows = rows_dev * lax.axis_size("lat")
    first_row = lax.axis_index("lat") * rows_dev - halo
    rows_ext = first_row + jnp.arange(rows_dev + 2 * halo)
    inside = ((rows_ext >= 0) & (rows_ext < total_rows))[:, None, None]
    stretch_rows = stretch(rows_ext, total_rows)
    gs_ext = expand(fields[..., :freqs_dev], spread)
    along_x = gs_ext * cos_head * stretch_rows[:, None, None]
    along_y = gs_ext * sin_head
    along_t = (
        expand(fields[..., freqs_dev : 2 * freqs_dev], spread) * sin_face
        - expand(fields[..., 2 * freqs_dev :], spread) * cos_face
    )
    for substep in range(ITERS):
        density = advect(density, along_x, 1)
        along_x, along_y, along_t = [trim(a, 1, 2) for a in (along_x, along_y, along_t)]
        density = advect(density, along_y, 0)
        inside = trim(inside, 0, 2)
        density = jnp.where(inside, density, 0.0)
        along_x, along_y, along_t = [trim(a, 0, 2) for a in (along_x, along_y, along_t)]
        density = refract(density, along_t)

    levels = jnp.exp(math.log(freq_ratio) * (comp_index // NDIR).astype(jnp.float32))
    ice_loss = lax.dynamic_slice_in_dim(jnp.repeat(ice_rate, NDIR), first_comp, comps_dev, 0)
    partial = jnp.stack([jnp.sum(density, axis=-1), jnp.sum(density * levels, axis=-1)])
    other = lax.ppermute(partial, "band", [(0, 1), (1, 0)])
    energy_sum = partial[0] + other[0]
    moment = partial[1] + other[1]
    return sources(
        density,
        energy_sum,
        moment,
        levels,
        heading,
        ice_loss,
        sea_share,
        ice_share,
        wind_speed,
        wind_dir,
    )


def solution(mesh):
    return jax.shard_map(
        per_device,
        mesh=mesh,
        in_specs=(
            P("lat", "lon", "band"),
            P("lat", "lon"),
            P("lat", "lon"),
            P("lat", "lon"),
            P(),
            P(),
            P(None, "lat", "lon"),
            P("lat", "lon"),
            P("lat", "lon"),
            P(),
        ),
        out_specs=P("lat", "lon", "band"),
        check_vma=False,
    )
```

```python
import functools
import math

import jax
import jax.numpy as jnp
from jax import lax
from jax.experimental import pallas as pl
from jax.experimental.pallas import tpu as pltpu
from jax.sharding import PartitionSpec as P

NDIR = 36
ITERS = 4
NCOMP = 576


freq_ratio = 1.1
wind_gain = 0.12
break_coef = 0.05
south_edge = -30.0
band_span = 60.0


def quickest(behind, center, forward, beyond, courant):
    curvature = jnp.where(
        courant >= 0.0, forward - 2.0 * center + behind, beyond - 2.0 * forward + center
    )
    face_value = (
        0.5 * (center + forward)
        - 0.5 * courant * (forward - center)
        - (1.0 - courant * courant) / 6.0 * curvature
    )
    return courant * face_value


def advect(density, cell_speed, axis_dim):
    length = density.shape[axis_dim]

    def piece(array, low, high):
        return lax.slice_in_dim(array, low, high, axis=axis_dim)

    courant = 0.5 * (piece(cell_speed, 1, length - 2) + piece(cell_speed, 2, length - 1))
    fluxes = quickest(
        piece(density, 0, length - 3),
        piece(density, 1, length - 2),
        piece(density, 2, length - 1),
        piece(density, 3, length),
        courant,
    )
    faces = fluxes.shape[axis_dim]
    return piece(density, 2, length - 2) - (piece(fluxes, 1, faces) - piece(fluxes, 0, faces - 1))


def shifted(density, offset):
    edges = [(0, 0, 0)] * (density.ndim - 1) + [(-offset, offset, 0)]
    return lax.pad(density, jnp.zeros((), density.dtype), edges)


def rotate(density, offset):
    dir_index = jnp.arange(density.shape[-1]) % NDIR
    target = dir_index + offset
    inner = shifted(density, offset)
    if offset > 0:
        return jnp.where(target >= NDIR, shifted(density, offset - NDIR), inner)
    return jnp.where(target < 0, shifted(density, offset + NDIR), inner)


def refract(density, courant):
    fluxes = quickest(rotate(density, -1), density, rotate(density, 1), rotate(density, 2), courant)
    return density - (fluxes - rotate(fluxes, -1))


def expand(per_freq, spread):
    total = jnp.where(spread[0] > 0.5, per_freq[..., 0:1], 0.0)
    for freq in range(1, spread.shape[0]):
        total = total + jnp.where(spread[freq] > 0.5, per_freq[..., freq : freq + 1], 0.0)
    return total


def lookup(classes, lookup_table):
    onehot = (classes[..., None] == jnp.arange(lookup_table.shape[0])).astype(jnp.float32)
    return jnp.dot(onehot, lookup_table, precision=lax.Precision.HIGHEST)


def stretch(rows, total_rows):
    latitude = (south_edge + band_span * (rows.astype(jnp.float32) + 0.5) / total_rows) * (
        math.pi / 180.0
    )
    return 1.0 / jnp.cos(latitude)


def sources(
    density,
    energy_sum,
    moment,
    levels,
    heading,
    ice_loss,
    sea_share,
    ice_share,
    wind_speed,
    wind_dir,
):
    mean_level = jnp.maximum(moment, 1.0) / jnp.maximum(energy_sum, 1.0)
    energy = energy_sum / NCOMP
    breaking = break_coef * levels * levels / mean_level[..., None] * (energy * energy)[..., None]
    growth = (
        wind_gain
        * wind_speed[..., None]
        * levels
        * jnp.maximum(jnp.cos(heading - wind_dir[..., None]), 0.0)
    )
    damping = ice_share[..., None] * ice_loss
    return sea_share[..., None] * density * jnp.exp(growth - breaking - damping)


INTERPRET = False
MESH_ID = pl.DeviceIdType.MESH
OFFSETS = [(a, b) for a in (-1, 0, 1) for b in (-1, 0, 1) if (a, b) != (0, 0)]


def halo_kernel(in_ref, out_ref, send_sem, recv_sem, *, halo):
    lon = lax.axis_index("lon")
    lat = lax.axis_index("lat")
    nlon = lax.axis_size("lon")
    nlat = lax.axis_size("lat")
    rows, cols = in_ref.shape[:2]

    def target(a, b):
        return {"lon": lax.rem(lon + b + nlon, nlon), "lat": lat + a}

    def has(a):
        return jnp.logical_and(lat + a >= 0, lat + a < nlat)

    def span(a, size):
        if a == 1:
            return pl.ds(size - halo, halo), pl.ds(0, halo)
        if a == -1:
            return pl.ds(0, halo), pl.ds(size + halo, halo)
        return pl.ds(0, size), pl.ds(halo, size)

    barrier = pltpu.get_barrier_semaphore()
    for a, b in OFFSETS:

        @pl.when(has(a))
        def _():
            pl.semaphore_signal(barrier, inc=1, device_id=target(a, b), device_id_type=MESH_ID)

    below = (lat + nlat - 1) // nlat
    above = 1 - lat // (nlat - 1)
    pl.semaphore_wait(barrier, 3 * (1 + below + above) - 1)

    copies = []
    for k, (a, b) in enumerate(OFFSETS):
        rows_src, rows_dst = span(a, rows)
        cols_src, cols_dst = span(b, cols)
        copy = pltpu.make_async_remote_copy(
            src_ref=in_ref.at[rows_src, cols_src],
            dst_ref=out_ref.at[rows_dst, cols_dst],
            send_sem=send_sem.at[k],
            recv_sem=recv_sem.at[k],
            device_id=target(a, b),
            device_id_type=MESH_ID,
        )
        pl.when(has(a))(copy.start)
        copies.append((a, copy))

    out_ref[pl.ds(halo, rows), pl.ds(halo, cols)] = in_ref[...]
    ghost = jnp.zeros((halo,) + out_ref.shape[1:], out_ref.dtype)

    @pl.when(lat == 0)
    def _():
        out_ref[pl.ds(0, halo)] = ghost

    @pl.when(lat == nlat - 1)
    def _():
        out_ref[pl.ds(rows + halo, halo)] = ghost

    for a, copy in copies:
        pl.when(has(a))(copy.wait_send)
        pl.when(has(-a))(copy.wait_recv)


def halo_exchange(cells, halo):
    rows, cols, chans = cells.shape
    vmem = pl.BlockSpec(memory_space=pltpu.VMEM)
    return pl.pallas_call(
        functools.partial(halo_kernel, halo=halo),
        out_shape=jax.ShapeDtypeStruct((rows + 2 * halo, cols + 2 * halo, chans), cells.dtype),
        in_specs=[vmem],
        out_specs=vmem,
        scratch_shapes=[pltpu.SemaphoreType.DMA((8,)), pltpu.SemaphoreType.DMA((8,))],
        compiler_params=pltpu.CompilerParams(collective_id=0, has_side_effects=True),
        interpret=pltpu.InterpretParams(detect_races=True) if INTERPRET else False,
    )(cells)


def exchange(cells, axis, dim, width, closed):
    count = lax.axis_size(axis)
    ends = count if closed else count - 1
    head = lax.slice_in_dim(cells, 0, width, axis=dim)
    tail = lax.slice_in_dim(cells, cells.shape[dim] - width, cells.shape[dim], axis=dim)
    before = lax.ppermute(tail, axis, [(i, (i + 1) % count) for i in range(ends)])
    after = lax.ppermute(head, axis, [((i + 1) % count, i) for i in range(ends)])
    return jnp.concatenate([before, cells, after], axis=dim)


def trim(array, dim, amount):
    return lax.slice_in_dim(array, amount, array.shape[dim] - amount, axis=dim)


def per_device(
    spectrum,
    sea_mask,
    ice_mask,
    depth_class,
    speed_table,
    refraction_table,
    depth_slope,
    wind_speed,
    wind_dir,
    ice_rate,
):
    rows_dev, cols_dev, comps_dev = spectrum.shape
    freqs_dev = comps_dev // NDIR
    halo = 2 * ITERS
    band_index = lax.axis_index("band")
    first_comp = band_index * comps_dev
    local_comp = jnp.arange(comps_dev)
    comp_index = first_comp + local_comp
    spread = (local_comp[None, :] // NDIR == jnp.arange(freqs_dev)[:, None]).astype(jnp.float32)
    heading = 2.0 * math.pi * (comp_index % NDIR).astype(jnp.float32) / NDIR
    face_angle = heading + math.pi / NDIR
    cos_head = jnp.cos(heading)
    sin_head = jnp.sin(heading)
    sin_face = jnp.sin(face_angle)
    cos_face = jnp.cos(face_angle)
    sea_share = sea_mask.astype(jnp.float32)
    ice_share = ice_mask.astype(jnp.float32)
    speed_local = lax.dynamic_slice_in_dim(speed_table, band_index * freqs_dev, freqs_dev, 1)
    refr_local = lax.dynamic_slice_in_dim(refraction_table, band_index * freqs_dev, freqs_dev, 1)
    chosen = (depth_class[..., None] == jnp.arange(speed_table.shape[0]))[..., None]
    group_speed = jnp.sum(jnp.where(chosen, speed_local, 0.0), axis=2) * sea_share[..., None]
    turning = jnp.sum(jnp.where(chosen, refr_local, 0.0), axis=2) * sea_share[..., None]
    turn_x = turning * depth_slope[0][..., None]
    turn_y = turning * depth_slope[1][..., None]
    density = spectrum * sea_share[..., None]

    stacked = jnp.concatenate([density, group_speed, turn_x, turn_y], axis=-1)
    stacked = halo_exchange(stacked, halo)
    density = stacked[..., :comps_dev]
    fields = stacked[..., comps_dev:]

    total_rows = rows_dev * lax.axis_size("lat")
    first_row = lax.axis_index("lat") * rows_dev - halo
    rows_ext = first_row + jnp.arange(rows_dev + 2 * halo)
    inside = ((rows_ext >= 0) & (rows_ext < total_rows))[:, None, None]
    stretch_rows = stretch(rows_ext, total_rows)
    gs_ext = expand(fields[..., :freqs_dev], spread)
    along_x = gs_ext * cos_head * stretch_rows[:, None, None]
    along_y = gs_ext * sin_head
    along_t = (
        expand(fields[..., freqs_dev : 2 * freqs_dev], spread) * sin_face
        - expand(fields[..., 2 * freqs_dev :], spread) * cos_face
    )
    for substep in range(ITERS):
        density = advect(density, along_x, 1)
        along_x, along_y, along_t = [trim(a, 1, 2) for a in (along_x, along_y, along_t)]
        density = advect(density, along_y, 0)
        inside = trim(inside, 0, 2)
        density = jnp.where(inside, density, 0.0)
        along_x, along_y, along_t = [trim(a, 0, 2) for a in (along_x, along_y, along_t)]
        density = refract(density, along_t)

    levels = jnp.exp(math.log(freq_ratio) * (comp_index // NDIR).astype(jnp.float32))
    ice_loss = lax.dynamic_slice_in_dim(jnp.repeat(ice_rate, NDIR), first_comp, comps_dev, 0)
    partial = jnp.stack([jnp.sum(density, axis=-1), jnp.sum(density * levels, axis=-1)])
    other = lax.ppermute(partial, "band", [(0, 1), (1, 0)])
    energy_sum = partial[0] + other[0]
    moment = partial[1] + other[1]
    return sources(
        density,
        energy_sum,
        moment,
        levels,
        heading,
        ice_loss,
        sea_share,
        ice_share,
        wind_speed,
        wind_dir,
    )


def solution(mesh):
    return jax.shard_map(
        per_device,
        mesh=mesh,
        in_specs=(
            P("lat", "lon", "band"),
            P("lat", "lon"),
            P("lat", "lon"),
            P("lat", "lon"),
            P(),
            P(),
            P(None, "lat", "lon"),
            P("lat", "lon"),
            P("lat", "lon"),
            P(),
        ),
        out_specs=P("lat", "lon", "band"),
        check_vma=False,
    )
```

```python
import functools
import math

import jax
import jax.numpy as jnp
from jax import lax
from jax.experimental import pallas as pl
from jax.experimental.pallas import tpu as pltpu
from jax.sharding import PartitionSpec as P

NDIR = 36
ITERS = 4
NCOMP = 576


freq_ratio = 1.1
wind_gain = 0.12
break_coef = 0.05
south_edge = -30.0
band_span = 60.0


def quickest(behind, center, forward, beyond, courant):
    curvature = jnp.where(
        courant >= 0.0, forward - 2.0 * center + behind, beyond - 2.0 * forward + center
    )
    face_value = (
        0.5 * (center + forward)
        - 0.5 * courant * (forward - center)
        - (1.0 - courant * courant) / 6.0 * curvature
    )
    return courant * face_value


def advect(density, cell_speed, axis_dim):
    length = density.shape[axis_dim]

    def piece(array, low, high):
        return lax.slice_in_dim(array, low, high, axis=axis_dim)

    courant = 0.5 * (piece(cell_speed, 1, length - 2) + piece(cell_speed, 2, length - 1))
    fluxes = quickest(
        piece(density, 0, length - 3),
        piece(density, 1, length - 2),
        piece(density, 2, length - 1),
        piece(density, 3, length),
        courant,
    )
    faces = fluxes.shape[axis_dim]
    return piece(density, 2, length - 2) - (piece(fluxes, 1, faces) - piece(fluxes, 0, faces - 1))


def shifted(density, offset):
    edges = [(0, 0, 0)] * (density.ndim - 1) + [(-offset, offset, 0)]
    return lax.pad(density, jnp.zeros((), density.dtype), edges)


def rotate(density, offset):
    dir_index = jnp.arange(density.shape[-1]) % NDIR
    target = dir_index + offset
    inner = shifted(density, offset)
    if offset > 0:
        return jnp.where(target >= NDIR, shifted(density, offset - NDIR), inner)
    return jnp.where(target < 0, shifted(density, offset + NDIR), inner)


def refract(density, courant):
    fluxes = quickest(rotate(density, -1), density, rotate(density, 1), rotate(density, 2), courant)
    return density - (fluxes - rotate(fluxes, -1))


def expand(per_freq, spread):
    return jnp.dot(per_freq, spread, precision=lax.Precision.HIGHEST)


def lookup(classes, lookup_table):
    onehot = (classes[..., None] == jnp.arange(lookup_table.shape[0])).astype(jnp.float32)
    return jnp.dot(onehot, lookup_table, precision=lax.Precision.HIGHEST)


def stretch(rows, total_rows):
    latitude = (south_edge + band_span * (rows.astype(jnp.float32) + 0.5) / total_rows) * (
        math.pi / 180.0
    )
    return 1.0 / jnp.cos(latitude)


def sources(
    density,
    energy_sum,
    moment,
    levels,
    heading,
    ice_loss,
    sea_share,
    ice_share,
    wind_speed,
    wind_dir,
):
    mean_level = jnp.maximum(moment, 1.0) / jnp.maximum(energy_sum, 1.0)
    energy = energy_sum / NCOMP
    breaking = break_coef * levels * levels / mean_level[..., None] * (energy * energy)[..., None]
    alignment = (
        jnp.cos(heading) * jnp.cos(wind_dir)[..., None]
        + jnp.sin(heading) * jnp.sin(wind_dir)[..., None]
    )
    growth = wind_gain * wind_speed[..., None] * levels * jnp.maximum(alignment, 0.0)
    damping = ice_share[..., None] * ice_loss
    return sea_share[..., None] * density * jnp.exp(growth - breaking - damping)


INTERPRET = False
MESH_ID = pl.DeviceIdType.MESH
OFFSETS = [(a, b) for a in (-1, 0, 1) for b in (-1, 0, 1) if (a, b) != (0, 0)]


def halo_kernel(in_ref, out_ref, send_sem, recv_sem, *, halo):
    lon = lax.axis_index("lon")
    lat = lax.axis_index("lat")
    nlon = lax.axis_size("lon")
    nlat = lax.axis_size("lat")
    rows, cols = in_ref.shape[:2]

    def target(a, b):
        return {"lon": lax.rem(lon + b + nlon, nlon), "lat": lat + a}

    def has(a):
        return jnp.logical_and(lat + a >= 0, lat + a < nlat)

    def span(a, size):
        if a == 1:
            return pl.ds(size - halo, halo), pl.ds(0, halo)
        if a == -1:
            return pl.ds(0, halo), pl.ds(size + halo, halo)
        return pl.ds(0, size), pl.ds(halo, size)

    barrier = pltpu.get_barrier_semaphore()
    for a, b in OFFSETS:

        @pl.when(has(a))
        def _():
            pl.semaphore_signal(barrier, inc=1, device_id=target(a, b), device_id_type=MESH_ID)

    below = (lat + nlat - 1) // nlat
    above = 1 - lat // (nlat - 1)
    pl.semaphore_wait(barrier, 3 * (1 + below + above) - 1)

    copies = []
    for k, (a, b) in enumerate(OFFSETS):
        rows_src, rows_dst = span(a, rows)
        cols_src, cols_dst = span(b, cols)
        copy = pltpu.make_async_remote_copy(
            src_ref=in_ref.at[rows_src, cols_src],
            dst_ref=out_ref.at[rows_dst, cols_dst],
            send_sem=send_sem.at[k],
            recv_sem=recv_sem.at[k],
            device_id=target(a, b),
            device_id_type=MESH_ID,
        )
        pl.when(has(a))(copy.start)
        copies.append((a, copy))

    out_ref[pl.ds(halo, rows), pl.ds(halo, cols)] = in_ref[...]
    ghost = jnp.zeros((halo,) + out_ref.shape[1:], out_ref.dtype)

    @pl.when(lat == 0)
    def _():
        out_ref[pl.ds(0, halo)] = ghost

    @pl.when(lat == nlat - 1)
    def _():
        out_ref[pl.ds(rows + halo, halo)] = ghost

    for a, copy in copies:
        pl.when(has(a))(copy.wait_send)
        pl.when(has(-a))(copy.wait_recv)


def halo_exchange(cells, halo):
    rows, cols, chans = cells.shape
    vmem = pl.BlockSpec(memory_space=pltpu.VMEM)
    return pl.pallas_call(
        functools.partial(halo_kernel, halo=halo),
        out_shape=jax.ShapeDtypeStruct((rows + 2 * halo, cols + 2 * halo, chans), cells.dtype),
        in_specs=[vmem],
        out_specs=vmem,
        scratch_shapes=[pltpu.SemaphoreType.DMA((8,)), pltpu.SemaphoreType.DMA((8,))],
        compiler_params=pltpu.CompilerParams(collective_id=0, has_side_effects=True),
        interpret=pltpu.InterpretParams(detect_races=True) if INTERPRET else False,
    )(cells)


def exchange(cells, axis, dim, width, closed):
    count = lax.axis_size(axis)
    ends = count if closed else count - 1
    head = lax.slice_in_dim(cells, 0, width, axis=dim)
    tail = lax.slice_in_dim(cells, cells.shape[dim] - width, cells.shape[dim], axis=dim)
    before = lax.ppermute(tail, axis, [(i, (i + 1) % count) for i in range(ends)])
    after = lax.ppermute(head, axis, [((i + 1) % count, i) for i in range(ends)])
    return jnp.concatenate([before, cells, after], axis=dim)


def trim(array, dim, amount):
    return lax.slice_in_dim(array, amount, array.shape[dim] - amount, axis=dim)


def per_device(
    spectrum,
    sea_mask,
    ice_mask,
    depth_class,
    speed_table,
    refraction_table,
    depth_slope,
    wind_speed,
    wind_dir,
    ice_rate,
):
    rows_dev, cols_dev, comps_dev = spectrum.shape
    freqs_dev = comps_dev // NDIR
    halo = 2 * ITERS
    band_index = lax.axis_index("band")
    first_comp = band_index * comps_dev
    local_comp = jnp.arange(comps_dev)
    comp_index = first_comp + local_comp
    spread = (local_comp[None, :] // NDIR == jnp.arange(freqs_dev)[:, None]).astype(jnp.float32)
    heading = 2.0 * math.pi * (comp_index % NDIR).astype(jnp.float32) / NDIR
    face_angle = heading + math.pi / NDIR
    cos_head = jnp.cos(heading)
    sin_head = jnp.sin(heading)
    sin_face = jnp.sin(face_angle)
    cos_face = jnp.cos(face_angle)
    sea_share = sea_mask.astype(jnp.float32)
    ice_share = ice_mask.astype(jnp.float32)
    speed_local = lax.dynamic_slice_in_dim(speed_table, band_index * freqs_dev, freqs_dev, 1)
    refr_local = lax.dynamic_slice_in_dim(refraction_table, band_index * freqs_dev, freqs_dev, 1)
    chosen = (depth_class[..., None] == jnp.arange(speed_table.shape[0]))[..., None]
    group_speed = jnp.sum(jnp.where(chosen, speed_local, 0.0), axis=2) * sea_share[..., None]
    turning = jnp.sum(jnp.where(chosen, refr_local, 0.0), axis=2) * sea_share[..., None]
    turn_x = turning * depth_slope[0][..., None]
    turn_y = turning * depth_slope[1][..., None]
    density = spectrum * sea_share[..., None]

    stacked = jnp.concatenate([density, group_speed, turn_x, turn_y], axis=-1)
    stacked = halo_exchange(stacked, halo)
    density = stacked[..., :comps_dev]
    fields = stacked[..., comps_dev:]

    total_rows = rows_dev * lax.axis_size("lat")
    first_row = lax.axis_index("lat") * rows_dev - halo
    rows_ext = first_row + jnp.arange(rows_dev + 2 * halo)
    inside = ((rows_ext >= 0) & (rows_ext < total_rows))[:, None, None]
    stretch_rows = stretch(rows_ext, total_rows)
    gs_ext = expand(fields[..., :freqs_dev], spread)
    along_x = gs_ext * cos_head * stretch_rows[:, None, None]
    along_y = gs_ext * sin_head
    along_t = (
        expand(fields[..., freqs_dev : 2 * freqs_dev], spread) * sin_face
        - expand(fields[..., 2 * freqs_dev :], spread) * cos_face
    )
    for substep in range(ITERS):
        density = advect(density, along_x, 1)
        along_x, along_y, along_t = [trim(a, 1, 2) for a in (along_x, along_y, along_t)]
        density = advect(density, along_y, 0)
        inside = trim(inside, 0, 2)
        density = jnp.where(inside, density, 0.0)
        along_x, along_y, along_t = [trim(a, 0, 2) for a in (along_x, along_y, along_t)]
        density = refract(density, along_t)

    levels = jnp.exp(math.log(freq_ratio) * (comp_index // NDIR).astype(jnp.float32))
    ice_loss = lax.dynamic_slice_in_dim(jnp.repeat(ice_rate, NDIR), first_comp, comps_dev, 0)
    partial = jnp.stack([jnp.sum(density, axis=-1), jnp.sum(density * levels, axis=-1)])
    other = lax.ppermute(partial, "band", [(0, 1), (1, 0)])
    energy_sum = partial[0] + other[0]
    moment = partial[1] + other[1]
    return sources(
        density,
        energy_sum,
        moment,
        levels,
        heading,
        ice_loss,
        sea_share,
        ice_share,
        wind_speed,
        wind_dir,
    )


def solution(mesh):
    return jax.shard_map(
        per_device,
        mesh=mesh,
        in_specs=(
            P("lat", "lon", "band"),
            P("lat", "lon"),
            P("lat", "lon"),
            P("lat", "lon"),
            P(),
            P(),
            P(None, "lat", "lon"),
            P("lat", "lon"),
            P("lat", "lon"),
            P(),
        ),
        out_specs=P("lat", "lon", "band"),
        check_vma=False,
    )
```

```python
import functools
import math

import jax
import jax.numpy as jnp
from jax import lax
from jax.experimental import pallas as pl
from jax.experimental.pallas import tpu as pltpu
from jax.sharding import PartitionSpec as P

NDIR = 36
ITERS = 4
NCOMP = 576


freq_ratio = 1.1
wind_gain = 0.12
break_coef = 0.05
south_edge = -30.0
band_span = 60.0


def quickest(behind, center, forward, beyond, courant):
    curvature = jnp.where(
        courant >= 0.0, forward - 2.0 * center + behind, beyond - 2.0 * forward + center
    )
    face_value = (
        0.5 * (center + forward)
        - 0.5 * courant * (forward - center)
        - (1.0 - courant * courant) / 6.0 * curvature
    )
    return courant * face_value


def advect(density, cell_speed, axis_dim):
    length = density.shape[axis_dim]

    def piece(array, low, high):
        return lax.slice_in_dim(array, low, high, axis=axis_dim)

    courant = 0.5 * (piece(cell_speed, 1, length - 2) + piece(cell_speed, 2, length - 1))
    fluxes = quickest(
        piece(density, 0, length - 3),
        piece(density, 1, length - 2),
        piece(density, 2, length - 1),
        piece(density, 3, length),
        courant,
    )
    faces = fluxes.shape[axis_dim]
    return piece(density, 2, length - 2) - (piece(fluxes, 1, faces) - piece(fluxes, 0, faces - 1))


def shifted(density, offset):
    edges = [(0, 0, 0)] * (density.ndim - 1) + [(-offset, offset, 0)]
    return lax.pad(density, jnp.zeros((), density.dtype), edges)


def rotate(density, offset):
    dir_index = jnp.arange(density.shape[-1]) % NDIR
    target = dir_index + offset
    inner = shifted(density, offset)
    if offset > 0:
        return jnp.where(target >= NDIR, shifted(density, offset - NDIR), inner)
    return jnp.where(target < 0, shifted(density, offset + NDIR), inner)


def refract(density, courant):
    fluxes = quickest(rotate(density, -1), density, rotate(density, 1), rotate(density, 2), courant)
    return density - (fluxes - rotate(fluxes, -1))


def expand(per_freq, spread):
    return jnp.dot(per_freq, spread, precision=lax.Precision.HIGHEST)


def lookup(classes, lookup_table):
    onehot = (classes[..., None] == jnp.arange(lookup_table.shape[0])).astype(jnp.float32)
    return jnp.dot(onehot, lookup_table, precision=lax.Precision.HIGHEST)


def stretch(rows, total_rows):
    latitude = (south_edge + band_span * (rows.astype(jnp.float32) + 0.5) / total_rows) * (
        math.pi / 180.0
    )
    return 1.0 / jnp.cos(latitude)


def sources(
    density,
    energy_sum,
    moment,
    levels,
    heading,
    ice_loss,
    sea_share,
    ice_share,
    wind_speed,
    wind_dir,
):
    mean_level = jnp.maximum(moment, 1.0) / jnp.maximum(energy_sum, 1.0)
    energy = energy_sum / NCOMP
    breaking = break_coef * levels * levels / mean_level[..., None] * (energy * energy)[..., None]
    alignment = (
        jnp.cos(heading) * jnp.cos(wind_dir)[..., None]
        + jnp.sin(heading) * jnp.sin(wind_dir)[..., None]
    )
    growth = wind_gain * wind_speed[..., None] * levels * jnp.maximum(alignment, 0.0)
    damping = ice_share[..., None] * ice_loss
    return sea_share[..., None] * density * jnp.exp(growth - breaking - damping)


INTERPRET = False
MESH_ID = pl.DeviceIdType.MESH
OFFSETS = [(a, b) for a in (-1, 0, 1) for b in (-1, 0, 1) if (a, b) != (0, 0)]


def halo_kernel(in_ref, out_ref, send_sem, recv_sem, *, halo):
    lon = lax.axis_index("lon")
    lat = lax.axis_index("lat")
    nlon = lax.axis_size("lon")
    nlat = lax.axis_size("lat")
    rows, cols = in_ref.shape[:2]

    def target(a, b):
        return {"lon": lax.rem(lon + b + nlon, nlon), "lat": lat + a}

    def has(a):
        return jnp.logical_and(lat + a >= 0, lat + a < nlat)

    def span(a, size):
        if a == 1:
            return pl.ds(size - halo, halo), pl.ds(0, halo)
        if a == -1:
            return pl.ds(0, halo), pl.ds(size + halo, halo)
        return pl.ds(0, size), pl.ds(halo, size)

    barrier = pltpu.get_barrier_semaphore()
    for a, b in OFFSETS:

        @pl.when(has(a))
        def _():
            pl.semaphore_signal(barrier, inc=1, device_id=target(a, b), device_id_type=MESH_ID)

    below = (lat + nlat - 1) // nlat
    above = 1 - lat // (nlat - 1)
    pl.semaphore_wait(barrier, 3 * (1 + below + above) - 1)

    copies = []
    for k, (a, b) in enumerate(OFFSETS):
        rows_src, rows_dst = span(a, rows)
        cols_src, cols_dst = span(b, cols)
        copy = pltpu.make_async_remote_copy(
            src_ref=in_ref.at[rows_src, cols_src],
            dst_ref=out_ref.at[rows_dst, cols_dst],
            send_sem=send_sem.at[k],
            recv_sem=recv_sem.at[k],
            device_id=target(a, b),
            device_id_type=MESH_ID,
        )
        pl.when(has(a))(copy.start)
        copies.append((a, copy))

    out_ref[pl.ds(halo, rows), pl.ds(halo, cols)] = in_ref[...]
    ghost = jnp.zeros((halo,) + out_ref.shape[1:], out_ref.dtype)

    @pl.when(lat == 0)
    def _():
        out_ref[pl.ds(0, halo)] = ghost

    @pl.when(lat == nlat - 1)
    def _():
        out_ref[pl.ds(rows + halo, halo)] = ghost

    for a, copy in copies:
        pl.when(has(a))(copy.wait_send)
        pl.when(has(-a))(copy.wait_recv)


def halo_exchange(cells, halo):
    rows, cols, chans = cells.shape
    vmem = pl.BlockSpec(memory_space=pltpu.VMEM)
    return pl.pallas_call(
        functools.partial(halo_kernel, halo=halo),
        out_shape=jax.ShapeDtypeStruct((rows + 2 * halo, cols + 2 * halo, chans), cells.dtype),
        in_specs=[vmem],
        out_specs=vmem,
        scratch_shapes=[pltpu.SemaphoreType.DMA((8,)), pltpu.SemaphoreType.DMA((8,))],
        compiler_params=pltpu.CompilerParams(collective_id=0, has_side_effects=True),
        interpret=pltpu.InterpretParams(detect_races=True) if INTERPRET else False,
    )(cells)


def exchange(cells, axis, dim, width, closed):
    count = lax.axis_size(axis)
    ends = count if closed else count - 1
    head = lax.slice_in_dim(cells, 0, width, axis=dim)
    tail = lax.slice_in_dim(cells, cells.shape[dim] - width, cells.shape[dim], axis=dim)
    before = lax.ppermute(tail, axis, [(i, (i + 1) % count) for i in range(ends)])
    after = lax.ppermute(head, axis, [((i + 1) % count, i) for i in range(ends)])
    return jnp.concatenate([before, cells, after], axis=dim)


def trim(array, dim, amount):
    return lax.slice_in_dim(array, amount, array.shape[dim] - amount, axis=dim)


def per_device(
    spectrum,
    sea_mask,
    ice_mask,
    depth_class,
    speed_table,
    refraction_table,
    depth_slope,
    wind_speed,
    wind_dir,
    ice_rate,
):
    rows_dev, cols_dev, comps_dev = spectrum.shape
    freqs_dev = comps_dev // NDIR
    halo = 2 * ITERS
    band_index = lax.axis_index("band")
    first_comp = band_index * comps_dev
    local_comp = jnp.arange(comps_dev)
    comp_index = first_comp + local_comp
    spread = (local_comp[None, :] // NDIR == jnp.arange(freqs_dev)[:, None]).astype(jnp.float32)
    heading = 2.0 * math.pi * (comp_index % NDIR).astype(jnp.float32) / NDIR
    face_angle = heading + math.pi / NDIR
    cos_head = jnp.cos(heading)
    sin_head = jnp.sin(heading)
    sin_face = jnp.sin(face_angle)
    cos_face = jnp.cos(face_angle)
    sea_share = sea_mask.astype(jnp.float32)
    ice_share = ice_mask.astype(jnp.float32)
    speed_local = lax.dynamic_slice_in_dim(speed_table, band_index * freqs_dev, freqs_dev, 1)
    refr_local = lax.dynamic_slice_in_dim(refraction_table, band_index * freqs_dev, freqs_dev, 1)
    chosen = (depth_class[..., None] == jnp.arange(speed_table.shape[0]))[..., None]
    group_speed = jnp.sum(jnp.where(chosen, speed_local, 0.0), axis=2) * sea_share[..., None]
    turning = jnp.sum(jnp.where(chosen, refr_local, 0.0), axis=2) * sea_share[..., None]
    turn_x = turning * depth_slope[0][..., None]
    turn_y = turning * depth_slope[1][..., None]

    stacked = jnp.concatenate([spectrum, group_speed, turn_x, turn_y, sea_share[..., None]], axis=-1)
    stacked = halo_exchange(stacked, halo)
    density = stacked[..., :comps_dev] * stacked[..., -1:]
    fields = stacked[..., comps_dev:-1]

    total_rows = rows_dev * lax.axis_size("lat")
    first_row = lax.axis_index("lat") * rows_dev - halo
    rows_ext = first_row + jnp.arange(rows_dev + 2 * halo)
    inside = ((rows_ext >= 0) & (rows_ext < total_rows))[:, None, None]
    stretch_rows = stretch(rows_ext, total_rows)
    gs_ext = expand(fields[..., :freqs_dev], spread)
    along_x = gs_ext * cos_head * stretch_rows[:, None, None]
    along_y = gs_ext * sin_head
    along_t = (
        expand(fields[..., freqs_dev : 2 * freqs_dev], spread) * sin_face
        - expand(fields[..., 2 * freqs_dev :], spread) * cos_face
    )
    for substep in range(ITERS):
        density = advect(density, along_x, 1)
        along_x, along_y, along_t = [trim(a, 1, 2) for a in (along_x, along_y, along_t)]
        density = advect(density, along_y, 0)
        inside = trim(inside, 0, 2)
        density = jnp.where(inside, density, 0.0)
        along_x, along_y, along_t = [trim(a, 0, 2) for a in (along_x, along_y, along_t)]
        density = refract(density, along_t)

    levels = jnp.exp(math.log(freq_ratio) * (comp_index // NDIR).astype(jnp.float32))
    ice_loss = lax.dynamic_slice_in_dim(jnp.repeat(ice_rate, NDIR), first_comp, comps_dev, 0)
    partial = jnp.stack([jnp.sum(density, axis=-1), jnp.sum(density * levels, axis=-1)])
    other = lax.ppermute(partial, "band", [(0, 1), (1, 0)])
    energy_sum = partial[0] + other[0]
    moment = partial[1] + other[1]
    return sources(
        density,
        energy_sum,
        moment,
        levels,
        heading,
        ice_loss,
        sea_share,
        ice_share,
        wind_speed,
        wind_dir,
    )


def solution(mesh):
    return jax.shard_map(
        per_device,
        mesh=mesh,
        in_specs=(
            P("lat", "lon", "band"),
            P("lat", "lon"),
            P("lat", "lon"),
            P("lat", "lon"),
            P(),
            P(),
            P(None, "lat", "lon"),
            P("lat", "lon"),
            P("lat", "lon"),
            P(),
        ),
        out_specs=P("lat", "lon", "band"),
        check_vma=False,
    )
```

```python
import functools
import math

import jax
import jax.numpy as jnp
from jax import lax
from jax.experimental import pallas as pl
from jax.experimental.pallas import tpu as pltpu
from jax.sharding import PartitionSpec as P

NDIR = 36
ITERS = 4
NCOMP = 576


freq_ratio = 1.1
wind_gain = 0.12
break_coef = 0.05
south_edge = -30.0
band_span = 60.0


def quickest(behind, center, forward, beyond, courant):
    curvature = jnp.where(
        courant >= 0.0, forward - 2.0 * center + behind, beyond - 2.0 * forward + center
    )
    face_value = (
        0.5 * (center + forward)
        - 0.5 * courant * (forward - center)
        - (1.0 - courant * courant) / 6.0 * curvature
    )
    return courant * face_value


def advect(density, cell_speed, axis_dim):
    length = density.shape[axis_dim]

    def piece(array, low, high):
        return lax.slice_in_dim(array, low, high, axis=axis_dim)

    courant = 0.5 * (piece(cell_speed, 1, length - 2) + piece(cell_speed, 2, length - 1))
    fluxes = quickest(
        piece(density, 0, length - 3),
        piece(density, 1, length - 2),
        piece(density, 2, length - 1),
        piece(density, 3, length),
        courant,
    )
    faces = fluxes.shape[axis_dim]
    return piece(density, 2, length - 2) - (piece(fluxes, 1, faces) - piece(fluxes, 0, faces - 1))


def shifted(density, offset):
    edges = [(0, 0, 0)] * (density.ndim - 1) + [(-offset, offset, 0)]
    return lax.pad(density, jnp.zeros((), density.dtype), edges)


def rotate(density, offset):
    dir_index = jnp.arange(density.shape[-1]) % NDIR
    target = dir_index + offset
    inner = shifted(density, offset)
    if offset > 0:
        return jnp.where(target >= NDIR, shifted(density, offset - NDIR), inner)
    return jnp.where(target < 0, shifted(density, offset + NDIR), inner)


def refract(density, courant):
    fluxes = quickest(rotate(density, -1), density, rotate(density, 1), rotate(density, 2), courant)
    return density - (fluxes - rotate(fluxes, -1))


def expand(per_freq, spread):
    return jnp.dot(per_freq, spread, precision=lax.Precision.HIGHEST)


def lookup(classes, lookup_table):
    onehot = (classes[..., None] == jnp.arange(lookup_table.shape[0])).astype(jnp.float32)
    return jnp.dot(onehot, lookup_table, precision=lax.Precision.HIGHEST)


def stretch(rows, total_rows):
    latitude = (south_edge + band_span * (rows.astype(jnp.float32) + 0.5) / total_rows) * (
        math.pi / 180.0
    )
    return 1.0 / jnp.cos(latitude)


def sources(
    density,
    energy_sum,
    moment,
    levels,
    heading,
    ice_loss,
    sea_share,
    ice_share,
    wind_speed,
    wind_dir,
):
    mean_level = jnp.maximum(moment, 1.0) / jnp.maximum(energy_sum, 1.0)
    energy = energy_sum / NCOMP
    breaking = break_coef * levels * levels * ((energy * energy) / mean_level)[..., None]
    alignment = (
        jnp.cos(heading) * jnp.cos(wind_dir)[..., None]
        + jnp.sin(heading) * jnp.sin(wind_dir)[..., None]
    )
    growth = wind_gain * wind_speed[..., None] * levels * jnp.maximum(alignment, 0.0)
    damping = ice_share[..., None] * ice_loss
    return sea_share[..., None] * density * jnp.exp(growth - breaking - damping)


INTERPRET = False
MESH_ID = pl.DeviceIdType.MESH
OFFSETS = [(a, b) for a in (-1, 0, 1) for b in (-1, 0, 1) if (a, b) != (0, 0)]


def halo_kernel(in_ref, out_ref, send_sem, recv_sem, *, halo):
    lon = lax.axis_index("lon")
    lat = lax.axis_index("lat")
    nlon = lax.axis_size("lon")
    nlat = lax.axis_size("lat")
    rows, cols = in_ref.shape[:2]

    def target(a, b):
        return {"lon": lax.rem(lon + b + nlon, nlon), "lat": lat + a}

    def has(a):
        return jnp.logical_and(lat + a >= 0, lat + a < nlat)

    def span(a, size):
        if a == 1:
            return pl.ds(size - halo, halo), pl.ds(0, halo)
        if a == -1:
            return pl.ds(0, halo), pl.ds(size + halo, halo)
        return pl.ds(0, size), pl.ds(halo, size)

    barrier = pltpu.get_barrier_semaphore()
    for a, b in OFFSETS:

        @pl.when(has(a))
        def _():
            pl.semaphore_signal(barrier, inc=1, device_id=target(a, b), device_id_type=MESH_ID)

    below = (lat + nlat - 1) // nlat
    above = 1 - lat // (nlat - 1)
    pl.semaphore_wait(barrier, 3 * (1 + below + above) - 1)

    copies = []
    for k, (a, b) in enumerate(OFFSETS):
        rows_src, rows_dst = span(a, rows)
        cols_src, cols_dst = span(b, cols)
        copy = pltpu.make_async_remote_copy(
            src_ref=in_ref.at[rows_src, cols_src],
            dst_ref=out_ref.at[rows_dst, cols_dst],
            send_sem=send_sem.at[k],
            recv_sem=recv_sem.at[k],
            device_id=target(a, b),
            device_id_type=MESH_ID,
        )
        pl.when(has(a))(copy.start)
        copies.append((a, copy))

    out_ref[pl.ds(halo, rows), pl.ds(halo, cols)] = in_ref[...]
    ghost = jnp.zeros((halo,) + out_ref.shape[1:], out_ref.dtype)

    @pl.when(lat == 0)
    def _():
        out_ref[pl.ds(0, halo)] = ghost

    @pl.when(lat == nlat - 1)
    def _():
        out_ref[pl.ds(rows + halo, halo)] = ghost

    for a, copy in copies:
        pl.when(has(a))(copy.wait_send)
        pl.when(has(-a))(copy.wait_recv)


def halo_exchange(cells, halo):
    rows, cols, chans = cells.shape
    vmem = pl.BlockSpec(memory_space=pltpu.VMEM)
    return pl.pallas_call(
        functools.partial(halo_kernel, halo=halo),
        out_shape=jax.ShapeDtypeStruct((rows + 2 * halo, cols + 2 * halo, chans), cells.dtype),
        in_specs=[vmem],
        out_specs=vmem,
        scratch_shapes=[pltpu.SemaphoreType.DMA((8,)), pltpu.SemaphoreType.DMA((8,))],
        compiler_params=pltpu.CompilerParams(collective_id=0, has_side_effects=True),
        interpret=pltpu.InterpretParams(detect_races=True) if INTERPRET else False,
    )(cells)


def exchange(cells, axis, dim, width, closed):
    count = lax.axis_size(axis)
    ends = count if closed else count - 1
    head = lax.slice_in_dim(cells, 0, width, axis=dim)
    tail = lax.slice_in_dim(cells, cells.shape[dim] - width, cells.shape[dim], axis=dim)
    before = lax.ppermute(tail, axis, [(i, (i + 1) % count) for i in range(ends)])
    after = lax.ppermute(head, axis, [((i + 1) % count, i) for i in range(ends)])
    return jnp.concatenate([before, cells, after], axis=dim)


def trim(array, dim, amount):
    return lax.slice_in_dim(array, amount, array.shape[dim] - amount, axis=dim)


def per_device(
    spectrum,
    sea_mask,
    ice_mask,
    depth_class,
    speed_table,
    refraction_table,
    depth_slope,
    wind_speed,
    wind_dir,
    ice_rate,
):
    rows_dev, cols_dev, comps_dev = spectrum.shape
    freqs_dev = comps_dev // NDIR
    halo = 2 * ITERS
    band_index = lax.axis_index("band")
    first_comp = band_index * comps_dev
    local_comp = jnp.arange(comps_dev)
    comp_index = first_comp + local_comp
    spread = (local_comp[None, :] // NDIR == jnp.arange(freqs_dev)[:, None]).astype(jnp.float32)
    heading = 2.0 * math.pi * (comp_index % NDIR).astype(jnp.float32) / NDIR
    face_angle = heading + math.pi / NDIR
    cos_head = jnp.cos(heading)
    sin_head = jnp.sin(heading)
    sin_face = jnp.sin(face_angle)
    cos_face = jnp.cos(face_angle)
    sea_share = sea_mask.astype(jnp.float32)
    ice_share = ice_mask.astype(jnp.float32)
    speed_local = lax.dynamic_slice_in_dim(speed_table, band_index * freqs_dev, freqs_dev, 1)
    refr_local = lax.dynamic_slice_in_dim(refraction_table, band_index * freqs_dev, freqs_dev, 1)
    chosen = (depth_class[..., None] == jnp.arange(speed_table.shape[0]))[..., None]
    group_speed = jnp.sum(jnp.where(chosen, speed_local, 0.0), axis=2) * sea_share[..., None]
    turning = jnp.sum(jnp.where(chosen, refr_local, 0.0), axis=2) * sea_share[..., None]
    turn_x = turning * depth_slope[0][..., None]
    turn_y = turning * depth_slope[1][..., None]
    density = spectrum * sea_share[..., None]

    stacked = jnp.concatenate([density, group_speed, turn_x, turn_y], axis=-1)
    stacked = halo_exchange(stacked, halo)
    density = stacked[..., :comps_dev]
    fields = stacked[..., comps_dev:]

    total_rows = rows_dev * lax.axis_size("lat")
    first_row = lax.axis_index("lat") * rows_dev - halo
    rows_ext = first_row + jnp.arange(rows_dev + 2 * halo)
    inside = ((rows_ext >= 0) & (rows_ext < total_rows))[:, None, None]
    stretch_rows = stretch(rows_ext, total_rows)
    gs_ext = expand(fields[..., :freqs_dev], spread)
    along_x = gs_ext * cos_head * stretch_rows[:, None, None]
    along_y = gs_ext * sin_head
    along_t = (
        expand(fields[..., freqs_dev : 2 * freqs_dev], spread) * sin_face
        - expand(fields[..., 2 * freqs_dev :], spread) * cos_face
    )
    for substep in range(ITERS):
        density = advect(density, along_x, 1)
        along_x, along_y, along_t = [trim(a, 1, 2) for a in (along_x, along_y, along_t)]
        density = advect(density, along_y, 0)
        inside = trim(inside, 0, 2)
        density = jnp.where(inside, density, 0.0)
        along_x, along_y, along_t = [trim(a, 0, 2) for a in (along_x, along_y, along_t)]
        density = refract(density, along_t)

    levels = jnp.exp(math.log(freq_ratio) * (comp_index // NDIR).astype(jnp.float32))
    ice_loss = lax.dynamic_slice_in_dim(jnp.repeat(ice_rate, NDIR), first_comp, comps_dev, 0)
    partial = jnp.stack([jnp.sum(density, axis=-1), jnp.sum(density * levels, axis=-1)])
    other = lax.ppermute(partial, "band", [(0, 1), (1, 0)])
    energy_sum = partial[0] + other[0]
    moment = partial[1] + other[1]
    return sources(
        density,
        energy_sum,
        moment,
        levels,
        heading,
        ice_loss,
        sea_share,
        ice_share,
        wind_speed,
        wind_dir,
    )


def solution(mesh):
    return jax.shard_map(
        per_device,
        mesh=mesh,
        in_specs=(
            P("lat", "lon", "band"),
            P("lat", "lon"),
            P("lat", "lon"),
            P("lat", "lon"),
            P(),
            P(),
            P(None, "lat", "lon"),
            P("lat", "lon"),
            P("lat", "lon"),
            P(),
        ),
        out_specs=P("lat", "lon", "band"),
        check_vma=False,
    )
```

```python
import functools
import math

import jax
import jax.numpy as jnp
from jax import lax
from jax.experimental import pallas as pl
from jax.experimental.pallas import tpu as pltpu
from jax.sharding import PartitionSpec as P

NDIR = 36
ITERS = 4
NCOMP = 576


freq_ratio = 1.1
wind_gain = 0.12
break_coef = 0.05
south_edge = -30.0
band_span = 60.0


def quickest(behind, center, forward, beyond, courant):
    curvature = jnp.where(
        courant >= 0.0, forward - 2.0 * center + behind, beyond - 2.0 * forward + center
    )
    face_value = (
        0.5 * (center + forward)
        - 0.5 * courant * (forward - center)
        - (1.0 - courant * courant) / 6.0 * curvature
    )
    return courant * face_value


def advect(density, cell_speed, axis_dim):
    length = density.shape[axis_dim]

    def piece(array, low, high):
        return lax.slice_in_dim(array, low, high, axis=axis_dim)

    courant = 0.5 * (piece(cell_speed, 1, length - 2) + piece(cell_speed, 2, length - 1))
    fluxes = quickest(
        piece(density, 0, length - 3),
        piece(density, 1, length - 2),
        piece(density, 2, length - 1),
        piece(density, 3, length),
        courant,
    )
    faces = fluxes.shape[axis_dim]
    return piece(density, 2, length - 2) - (piece(fluxes, 1, faces) - piece(fluxes, 0, faces - 1))


def shifted(density, offset):
    edges = [(0, 0, 0)] * (density.ndim - 1) + [(-offset, offset, 0)]
    return lax.pad(density, jnp.zeros((), density.dtype), edges)


def rotate(density, offset):
    dir_index = jnp.arange(density.shape[-1]) % NDIR
    target = dir_index + offset
    inner = shifted(density, offset)
    if offset > 0:
        return jnp.where(target >= NDIR, shifted(density, offset - NDIR), inner)
    return jnp.where(target < 0, shifted(density, offset + NDIR), inner)


def refract(density, courant):
    fluxes = quickest(rotate(density, -1), density, rotate(density, 1), rotate(density, 2), courant)
    return density - (fluxes - rotate(fluxes, -1))


def expand(per_freq, spread):
    return jnp.dot(per_freq, spread, precision=lax.Precision.HIGH)


def lookup(classes, lookup_table):
    onehot = (classes[..., None] == jnp.arange(lookup_table.shape[0])).astype(jnp.float32)
    return jnp.dot(onehot, lookup_table, precision=lax.Precision.HIGHEST)


def stretch(rows, total_rows):
    latitude = (south_edge + band_span * (rows.astype(jnp.float32) + 0.5) / total_rows) * (
        math.pi / 180.0
    )
    return 1.0 / jnp.cos(latitude)


def sources(
    density,
    energy_sum,
    moment,
    levels,
    heading,
    ice_loss,
    sea_share,
    ice_share,
    wind_speed,
    wind_dir,
):
    mean_level = jnp.maximum(moment, 1.0) / jnp.maximum(energy_sum, 1.0)
    energy = energy_sum / NCOMP
    breaking = break_coef * levels * levels / mean_level[..., None] * (energy * energy)[..., None]
    alignment = (
        jnp.cos(heading) * jnp.cos(wind_dir)[..., None]
        + jnp.sin(heading) * jnp.sin(wind_dir)[..., None]
    )
    growth = wind_gain * wind_speed[..., None] * levels * jnp.maximum(alignment, 0.0)
    damping = ice_share[..., None] * ice_loss
    return sea_share[..., None] * density * jnp.exp(growth - breaking - damping)


INTERPRET = False
MESH_ID = pl.DeviceIdType.MESH
OFFSETS = [(a, b) for a in (-1, 0, 1) for b in (-1, 0, 1) if (a, b) != (0, 0)]


def halo_kernel(in_ref, out_ref, send_sem, recv_sem, *, halo):
    lon = lax.axis_index("lon")
    lat = lax.axis_index("lat")
    nlon = lax.axis_size("lon")
    nlat = lax.axis_size("lat")
    rows, cols = in_ref.shape[:2]

    def target(a, b):
        return {"lon": lax.rem(lon + b + nlon, nlon), "lat": lat + a}

    def has(a):
        return jnp.logical_and(lat + a >= 0, lat + a < nlat)

    def span(a, size):
        if a == 1:
            return pl.ds(size - halo, halo), pl.ds(0, halo)
        if a == -1:
            return pl.ds(0, halo), pl.ds(size + halo, halo)
        return pl.ds(0, size), pl.ds(halo, size)

    barrier = pltpu.get_barrier_semaphore()
    for a, b in OFFSETS:

        @pl.when(has(a))
        def _():
            pl.semaphore_signal(barrier, inc=1, device_id=target(a, b), device_id_type=MESH_ID)

    below = (lat + nlat - 1) // nlat
    above = 1 - lat // (nlat - 1)
    pl.semaphore_wait(barrier, 3 * (1 + below + above) - 1)

    copies = []
    for k, (a, b) in enumerate(OFFSETS):
        rows_src, rows_dst = span(a, rows)
        cols_src, cols_dst = span(b, cols)
        copy = pltpu.make_async_remote_copy(
            src_ref=in_ref.at[rows_src, cols_src],
            dst_ref=out_ref.at[rows_dst, cols_dst],
            send_sem=send_sem.at[k],
            recv_sem=recv_sem.at[k],
            device_id=target(a, b),
            device_id_type=MESH_ID,
        )
        pl.when(has(a))(copy.start)
        copies.append((a, copy))

    out_ref[pl.ds(halo, rows), pl.ds(halo, cols)] = in_ref[...]
    ghost = jnp.zeros((halo,) + out_ref.shape[1:], out_ref.dtype)

    @pl.when(lat == 0)
    def _():
        out_ref[pl.ds(0, halo)] = ghost

    @pl.when(lat == nlat - 1)
    def _():
        out_ref[pl.ds(rows + halo, halo)] = ghost

    for a, copy in copies:
        pl.when(has(a))(copy.wait_send)
        pl.when(has(-a))(copy.wait_recv)


def halo_exchange(cells, halo):
    rows, cols, chans = cells.shape
    vmem = pl.BlockSpec(memory_space=pltpu.VMEM)
    return pl.pallas_call(
        functools.partial(halo_kernel, halo=halo),
        out_shape=jax.ShapeDtypeStruct((rows + 2 * halo, cols + 2 * halo, chans), cells.dtype),
        in_specs=[vmem],
        out_specs=vmem,
        scratch_shapes=[pltpu.SemaphoreType.DMA((8,)), pltpu.SemaphoreType.DMA((8,))],
        compiler_params=pltpu.CompilerParams(collective_id=0, has_side_effects=True),
        interpret=pltpu.InterpretParams(detect_races=True) if INTERPRET else False,
    )(cells)


def exchange(cells, axis, dim, width, closed):
    count = lax.axis_size(axis)
    ends = count if closed else count - 1
    head = lax.slice_in_dim(cells, 0, width, axis=dim)
    tail = lax.slice_in_dim(cells, cells.shape[dim] - width, cells.shape[dim], axis=dim)
    before = lax.ppermute(tail, axis, [(i, (i + 1) % count) for i in range(ends)])
    after = lax.ppermute(head, axis, [((i + 1) % count, i) for i in range(ends)])
    return jnp.concatenate([before, cells, after], axis=dim)


def trim(array, dim, amount):
    return lax.slice_in_dim(array, amount, array.shape[dim] - amount, axis=dim)


def per_device(
    spectrum,
    sea_mask,
    ice_mask,
    depth_class,
    speed_table,
    refraction_table,
    depth_slope,
    wind_speed,
    wind_dir,
    ice_rate,
):
    rows_dev, cols_dev, comps_dev = spectrum.shape
    freqs_dev = comps_dev // NDIR
    halo = 2 * ITERS
    band_index = lax.axis_index("band")
    first_comp = band_index * comps_dev
    local_comp = jnp.arange(comps_dev)
    comp_index = first_comp + local_comp
    spread = (local_comp[None, :] // NDIR == jnp.arange(freqs_dev)[:, None]).astype(jnp.float32)
    heading = 2.0 * math.pi * (comp_index % NDIR).astype(jnp.float32) / NDIR
    face_angle = heading + math.pi / NDIR
    cos_head = jnp.cos(heading)
    sin_head = jnp.sin(heading)
    sin_face = jnp.sin(face_angle)
    cos_face = jnp.cos(face_angle)
    sea_share = sea_mask.astype(jnp.float32)
    ice_share = ice_mask.astype(jnp.float32)
    speed_local = lax.dynamic_slice_in_dim(speed_table, band_index * freqs_dev, freqs_dev, 1)
    refr_local = lax.dynamic_slice_in_dim(refraction_table, band_index * freqs_dev, freqs_dev, 1)
    chosen = (depth_class[..., None] == jnp.arange(speed_table.shape[0]))[..., None]
    group_speed = jnp.sum(jnp.where(chosen, speed_local, 0.0), axis=2) * sea_share[..., None]
    turning = jnp.sum(jnp.where(chosen, refr_local, 0.0), axis=2) * sea_share[..., None]
    turn_x = turning * depth_slope[0][..., None]
    turn_y = turning * depth_slope[1][..., None]
    density = spectrum * sea_share[..., None]

    stacked = jnp.concatenate([density, group_speed, turn_x, turn_y], axis=-1)
    stacked = halo_exchange(stacked, halo)
    density = stacked[..., :comps_dev]
    fields = stacked[..., comps_dev:]

    total_rows = rows_dev * lax.axis_size("lat")
    first_row = lax.axis_index("lat") * rows_dev - halo
    rows_ext = first_row + jnp.arange(rows_dev + 2 * halo)
    inside = ((rows_ext >= 0) & (rows_ext < total_rows))[:, None, None]
    stretch_rows = stretch(rows_ext, total_rows)
    gs_ext = expand(fields[..., :freqs_dev], spread)
    along_x = gs_ext * cos_head * stretch_rows[:, None, None]
    along_y = gs_ext * sin_head
    along_t = (
        expand(fields[..., freqs_dev : 2 * freqs_dev], spread) * sin_face
        - expand(fields[..., 2 * freqs_dev :], spread) * cos_face
    )
    for substep in range(ITERS):
        density = advect(density, along_x, 1)
        along_x, along_y, along_t = [trim(a, 1, 2) for a in (along_x, along_y, along_t)]
        density = advect(density, along_y, 0)
        inside = trim(inside, 0, 2)
        density = jnp.where(inside, density, 0.0)
        along_x, along_y, along_t = [trim(a, 0, 2) for a in (along_x, along_y, along_t)]
        density = refract(density, along_t)

    levels = jnp.exp(math.log(freq_ratio) * (comp_index // NDIR).astype(jnp.float32))
    ice_loss = lax.dynamic_slice_in_dim(jnp.repeat(ice_rate, NDIR), first_comp, comps_dev, 0)
    partial = jnp.stack([jnp.sum(density, axis=-1), jnp.sum(density * levels, axis=-1)])
    other = lax.ppermute(partial, "band", [(0, 1), (1, 0)])
    energy_sum = partial[0] + other[0]
    moment = partial[1] + other[1]
    return sources(
        density,
        energy_sum,
        moment,
        levels,
        heading,
        ice_loss,
        sea_share,
        ice_share,
        wind_speed,
        wind_dir,
    )


def solution(mesh):
    return jax.shard_map(
        per_device,
        mesh=mesh,
        in_specs=(
            P("lat", "lon", "band"),
            P("lat", "lon"),
            P("lat", "lon"),
            P("lat", "lon"),
            P(),
            P(),
            P(None, "lat", "lon"),
            P("lat", "lon"),
            P("lat", "lon"),
            P(),
        ),
        out_specs=P("lat", "lon", "band"),
        check_vma=False,
    )
```

```python
import functools
import math

import jax
import jax.numpy as jnp
from jax import lax
from jax.experimental import pallas as pl
from jax.experimental.pallas import tpu as pltpu
from jax.sharding import PartitionSpec as P

NDIR = 36
ITERS = 4
NCOMP = 576


freq_ratio = 1.1
wind_gain = 0.12
break_coef = 0.05
south_edge = -30.0
band_span = 60.0


def quickest(behind, center, forward, beyond, courant):
    curvature = jnp.where(
        courant >= 0.0, forward - 2.0 * center + behind, beyond - 2.0 * forward + center
    )
    face_value = (
        0.5 * (center + forward)
        - 0.5 * courant * (forward - center)
        - (1.0 - courant * courant) / 6.0 * curvature
    )
    return courant * face_value


def advect(density, cell_speed, axis_dim):
    length = density.shape[axis_dim]

    def piece(array, low, high):
        return lax.slice_in_dim(array, low, high, axis=axis_dim)

    courant = 0.5 * (piece(cell_speed, 1, length - 2) + piece(cell_speed, 2, length - 1))
    fluxes = quickest(
        piece(density, 0, length - 3),
        piece(density, 1, length - 2),
        piece(density, 2, length - 1),
        piece(density, 3, length),
        courant,
    )
    faces = fluxes.shape[axis_dim]
    return piece(density, 2, length - 2) - (piece(fluxes, 1, faces) - piece(fluxes, 0, faces - 1))


def shifted(density, offset):
    edges = [(0, 0, 0)] * (density.ndim - 1) + [(-offset, offset, 0)]
    return lax.pad(density, jnp.zeros((), density.dtype), edges)


def rotate(density, offset):
    dir_index = jnp.arange(density.shape[-1]) % NDIR
    target = dir_index + offset
    inner = shifted(density, offset)
    if offset > 0:
        return jnp.where(target >= NDIR, shifted(density, offset - NDIR), inner)
    return jnp.where(target < 0, shifted(density, offset + NDIR), inner)


def refract(density, courant):
    fluxes = quickest(rotate(density, -1), density, rotate(density, 1), rotate(density, 2), courant)
    return density - (fluxes - rotate(fluxes, -1))


def expand(per_freq, spread):
    return jnp.dot(per_freq, spread, precision=lax.Precision.HIGH)


def lookup(classes, lookup_table):
    onehot = (classes[..., None] == jnp.arange(lookup_table.shape[0])).astype(jnp.float32)
    return jnp.dot(onehot, lookup_table, precision=lax.Precision.HIGHEST)


def stretch(rows, total_rows):
    latitude = (south_edge + band_span * (rows.astype(jnp.float32) + 0.5) / total_rows) * (
        math.pi / 180.0
    )
    return 1.0 / jnp.cos(latitude)


def sources(
    density,
    energy_sum,
    moment,
    levels,
    heading,
    ice_loss,
    sea_share,
    ice_share,
    wind_speed,
    wind_dir,
):
    mean_level = jnp.maximum(moment, 1.0) / jnp.maximum(energy_sum, 1.0)
    energy = energy_sum / NCOMP
    breaking = break_coef * levels * levels / mean_level[..., None] * (energy * energy)[..., None]
    alignment = (
        jnp.cos(heading) * jnp.cos(wind_dir)[..., None]
        + jnp.sin(heading) * jnp.sin(wind_dir)[..., None]
    )
    growth = wind_gain * wind_speed[..., None] * levels * jnp.maximum(alignment, 0.0)
    damping = ice_share[..., None] * ice_loss
    return sea_share[..., None] * density * jnp.exp(growth - breaking - damping)


INTERPRET = False
MESH_ID = pl.DeviceIdType.MESH
OFFSETS = [(-1, -1), (-1, 1), (1, -1), (1, 1), (-1, 0), (1, 0), (0, -1), (0, 1)]


def halo_kernel(in_ref, out_ref, send_sem, recv_sem, own_sem, *, halo):
    lon = lax.axis_index("lon")
    lat = lax.axis_index("lat")
    nlon = lax.axis_size("lon")
    nlat = lax.axis_size("lat")
    rows, cols = in_ref.shape[:2]

    def target(a, b):
        return {"lon": lax.rem(lon + b + nlon, nlon), "lat": lat + a}

    def has(a):
        return jnp.logical_and(lat + a >= 0, lat + a < nlat)

    def span(a, size):
        if a == 1:
            return pl.ds(size - halo, halo), pl.ds(0, halo)
        if a == -1:
            return pl.ds(0, halo), pl.ds(size + halo, halo)
        return pl.ds(0, size), pl.ds(halo, size)

    barrier = pltpu.get_barrier_semaphore()
    for a, b in OFFSETS:

        @pl.when(has(a))
        def _():
            pl.semaphore_signal(barrier, inc=1, device_id=target(a, b), device_id_type=MESH_ID)

    below = (lat + nlat - 1) // nlat
    above = 1 - lat // (nlat - 1)
    pl.semaphore_wait(barrier, 3 * (1 + below + above) - 1)

    copies = []
    for k, (a, b) in enumerate(OFFSETS):
        rows_src, rows_dst = span(a, rows)
        cols_src, cols_dst = span(b, cols)
        copy = pltpu.make_async_remote_copy(
            src_ref=in_ref.at[rows_src, cols_src],
            dst_ref=out_ref.at[rows_dst, cols_dst],
            send_sem=send_sem.at[k],
            recv_sem=recv_sem.at[k],
            device_id=target(a, b),
            device_id_type=MESH_ID,
        )
        pl.when(has(a))(copy.start)
        copies.append((a, copy))

    own = pltpu.make_async_copy(in_ref, out_ref.at[pl.ds(halo, rows), pl.ds(halo, cols)], own_sem)
    own.start()
    ghost = jnp.zeros((halo,) + out_ref.shape[1:], out_ref.dtype)

    @pl.when(lat == 0)
    def _():
        out_ref[pl.ds(0, halo)] = ghost

    @pl.when(lat == nlat - 1)
    def _():
        out_ref[pl.ds(rows + halo, halo)] = ghost

    for a, copy in copies:
        pl.when(has(a))(copy.wait_send)
        pl.when(has(-a))(copy.wait_recv)
    own.wait()


def halo_exchange(cells, halo):
    rows, cols, chans = cells.shape
    vmem = pl.BlockSpec(memory_space=pltpu.VMEM)
    return pl.pallas_call(
        functools.partial(halo_kernel, halo=halo),
        out_shape=jax.ShapeDtypeStruct((rows + 2 * halo, cols + 2 * halo, chans), cells.dtype),
        in_specs=[vmem],
        out_specs=vmem,
        scratch_shapes=[
            pltpu.SemaphoreType.DMA((8,)),
            pltpu.SemaphoreType.DMA((8,)),
            pltpu.SemaphoreType.DMA(()),
        ],
        compiler_params=pltpu.CompilerParams(collective_id=0, has_side_effects=True),
        interpret=pltpu.InterpretParams(detect_races=True) if INTERPRET else False,
    )(cells)


def exchange(cells, axis, dim, width, closed):
    count = lax.axis_size(axis)
    ends = count if closed else count - 1
    head = lax.slice_in_dim(cells, 0, width, axis=dim)
    tail = lax.slice_in_dim(cells, cells.shape[dim] - width, cells.shape[dim], axis=dim)
    before = lax.ppermute(tail, axis, [(i, (i + 1) % count) for i in range(ends)])
    after = lax.ppermute(head, axis, [((i + 1) % count, i) for i in range(ends)])
    return jnp.concatenate([before, cells, after], axis=dim)


def trim(array, dim, amount):
    return lax.slice_in_dim(array, amount, array.shape[dim] - amount, axis=dim)


def per_device(
    spectrum,
    sea_mask,
    ice_mask,
    depth_class,
    speed_table,
    refraction_table,
    depth_slope,
    wind_speed,
    wind_dir,
    ice_rate,
):
    rows_dev, cols_dev, comps_dev = spectrum.shape
    freqs_dev = comps_dev // NDIR
    halo = 2 * ITERS
    band_index = lax.axis_index("band")
    first_comp = band_index * comps_dev
    local_comp = jnp.arange(comps_dev)
    comp_index = first_comp + local_comp
    spread = (local_comp[None, :] // NDIR == jnp.arange(freqs_dev)[:, None]).astype(jnp.float32)
    heading = 2.0 * math.pi * (comp_index % NDIR).astype(jnp.float32) / NDIR
    face_angle = heading + math.pi / NDIR
    cos_head = jnp.cos(heading)
    sin_head = jnp.sin(heading)
    sin_face = jnp.sin(face_angle)
    cos_face = jnp.cos(face_angle)
    sea_share = sea_mask.astype(jnp.float32)
    ice_share = ice_mask.astype(jnp.float32)
    speed_local = lax.dynamic_slice_in_dim(speed_table, band_index * freqs_dev, freqs_dev, 1)
    refr_local = lax.dynamic_slice_in_dim(refraction_table, band_index * freqs_dev, freqs_dev, 1)
    chosen = (depth_class[..., None] == jnp.arange(speed_table.shape[0]))[..., None]
    group_speed = jnp.sum(jnp.where(chosen, speed_local, 0.0), axis=2) * sea_share[..., None]
    turning = jnp.sum(jnp.where(chosen, refr_local, 0.0), axis=2) * sea_share[..., None]
    turn_x = turning * depth_slope[0][..., None]
    turn_y = turning * depth_slope[1][..., None]
    density = spectrum * sea_share[..., None]

    stacked = jnp.concatenate([density, group_speed, turn_x, turn_y], axis=-1)
    stacked = halo_exchange(stacked, halo)
    density = stacked[..., :comps_dev]
    fields = stacked[..., comps_dev:]

    total_rows = rows_dev * lax.axis_size("lat")
    first_row = lax.axis_index("lat") * rows_dev - halo
    rows_ext = first_row + jnp.arange(rows_dev + 2 * halo)
    inside = ((rows_ext >= 0) & (rows_ext < total_rows))[:, None, None]
    stretch_rows = stretch(rows_ext, total_rows)
    gs_ext = expand(fields[..., :freqs_dev], spread)
    along_x = gs_ext * cos_head * stretch_rows[:, None, None]
    along_y = gs_ext * sin_head
    along_t = (
        expand(fields[..., freqs_dev : 2 * freqs_dev], spread) * sin_face
        - expand(fields[..., 2 * freqs_dev :], spread) * cos_face
    )
    for substep in range(ITERS):
        density = advect(density, along_x, 1)
        along_x, along_y, along_t = [trim(a, 1, 2) for a in (along_x, along_y, along_t)]
        density = advect(density, along_y, 0)
        inside = trim(inside, 0, 2)
        density = jnp.where(inside, density, 0.0)
        along_x, along_y, along_t = [trim(a, 0, 2) for a in (along_x, along_y, along_t)]
        density = refract(density, along_t)

    levels = jnp.exp(math.log(freq_ratio) * (comp_index // NDIR).astype(jnp.float32))
    ice_loss = lax.dynamic_slice_in_dim(jnp.repeat(ice_rate, NDIR), first_comp, comps_dev, 0)
    partial = jnp.stack([jnp.sum(density, axis=-1), jnp.sum(density * levels, axis=-1)])
    other = lax.ppermute(partial, "band", [(0, 1), (1, 0)])
    energy_sum = partial[0] + other[0]
    moment = partial[1] + other[1]
    return sources(
        density,
        energy_sum,
        moment,
        levels,
        heading,
        ice_loss,
        sea_share,
        ice_share,
        wind_speed,
        wind_dir,
    )


def solution(mesh):
    return jax.shard_map(
        per_device,
        mesh=mesh,
        in_specs=(
            P("lat", "lon", "band"),
            P("lat", "lon"),
            P("lat", "lon"),
            P("lat", "lon"),
            P(),
            P(),
            P(None, "lat", "lon"),
            P("lat", "lon"),
            P("lat", "lon"),
            P(),
        ),
        out_specs=P("lat", "lon", "band"),
        check_vma=False,
    )
```

```python
import functools
import math

import jax
import jax.numpy as jnp
from jax import lax
from jax.experimental import pallas as pl
from jax.experimental.pallas import tpu as pltpu
from jax.sharding import PartitionSpec as P

NDIR = 36
ITERS = 4
NCOMP = 576


freq_ratio = 1.1
wind_gain = 0.12
break_coef = 0.05
south_edge = -30.0
band_span = 60.0


def quickest(behind, center, forward, beyond, courant):
    curvature = jnp.where(
        courant >= 0.0, forward - 2.0 * center + behind, beyond - 2.0 * forward + center
    )
    face_value = (
        0.5 * (center + forward)
        - 0.5 * courant * (forward - center)
        - (1.0 - courant * courant) / 6.0 * curvature
    )
    return courant * face_value


def advect(density, cell_speed, axis_dim):
    length = density.shape[axis_dim]

    def piece(array, low, high):
        return lax.slice_in_dim(array, low, high, axis=axis_dim)

    courant = 0.5 * (piece(cell_speed, 1, length - 2) + piece(cell_speed, 2, length - 1))
    fluxes = quickest(
        piece(density, 0, length - 3),
        piece(density, 1, length - 2),
        piece(density, 2, length - 1),
        piece(density, 3, length),
        courant,
    )
    faces = fluxes.shape[axis_dim]
    return piece(density, 2, length - 2) - (piece(fluxes, 1, faces) - piece(fluxes, 0, faces - 1))


def shifted(density, offset):
    edges = [(0, 0, 0)] * (density.ndim - 1) + [(-offset, offset, 0)]
    return lax.pad(density, jnp.zeros((), density.dtype), edges)


def rotate(density, offset):
    dir_index = jnp.arange(density.shape[-1]) % NDIR
    target = dir_index + offset
    inner = shifted(density, offset)
    if offset > 0:
        return jnp.where(target >= NDIR, shifted(density, offset - NDIR), inner)
    return jnp.where(target < 0, shifted(density, offset + NDIR), inner)


def refract(density, courant):
    fluxes = quickest(rotate(density, -1), density, rotate(density, 1), rotate(density, 2), courant)
    return density - (fluxes - rotate(fluxes, -1))


def expand(per_freq, spread):
    return jnp.dot(per_freq, spread, precision=lax.Precision.HIGH)


def lookup(classes, lookup_table):
    onehot = (classes[..., None] == jnp.arange(lookup_table.shape[0])).astype(jnp.float32)
    return jnp.dot(onehot, lookup_table, precision=lax.Precision.HIGHEST)


def stretch(rows, total_rows):
    latitude = (south_edge + band_span * (rows.astype(jnp.float32) + 0.5) / total_rows) * (
        math.pi / 180.0
    )
    return 1.0 / jnp.cos(latitude)


def sources(
    density,
    energy_sum,
    moment,
    levels,
    heading,
    ice_loss,
    sea_share,
    ice_share,
    wind_speed,
    wind_dir,
):
    mean_level = jnp.maximum(moment, 1.0) / jnp.maximum(energy_sum, 1.0)
    energy = energy_sum / NCOMP
    breaking = break_coef * levels * levels / mean_level[..., None] * (energy * energy)[..., None]
    alignment = (
        jnp.cos(heading) * jnp.cos(wind_dir)[..., None]
        + jnp.sin(heading) * jnp.sin(wind_dir)[..., None]
    )
    growth = wind_gain * wind_speed[..., None] * levels * jnp.maximum(alignment, 0.0)
    damping = ice_share[..., None] * ice_loss
    return sea_share[..., None] * density * jnp.exp(growth - breaking - damping)


INTERPRET = False
MESH_ID = pl.DeviceIdType.MESH
OFFSETS = [(-1, -1), (-1, 1), (1, -1), (1, 1), (-1, 0), (1, 0), (0, -1), (0, 1)]


def halo_kernel(in_ref, out_ref, send_sem, recv_sem, own_sem, *, halo):
    lon = lax.axis_index("lon")
    lat = lax.axis_index("lat")
    nlon = lax.axis_size("lon")
    nlat = lax.axis_size("lat")
    rows, cols = in_ref.shape[:2]

    def target(a, b):
        return {"lon": lax.rem(lon + b + nlon, nlon), "lat": lat + a}

    def has(a):
        return jnp.logical_and(lat + a >= 0, lat + a < nlat)

    def span(a, size):
        if a == 1:
            return pl.ds(size - halo, halo), pl.ds(0, halo)
        if a == -1:
            return pl.ds(0, halo), pl.ds(size + halo, halo)
        return pl.ds(0, size), pl.ds(halo, size)

    barrier = pltpu.get_barrier_semaphore()
    for a, b in OFFSETS:

        @pl.when(has(a))
        def _():
            pl.semaphore_signal(barrier, inc=1, device_id=target(a, b), device_id_type=MESH_ID)

    below = (lat + nlat - 1) // nlat
    above = 1 - lat // (nlat - 1)
    pl.semaphore_wait(barrier, 3 * (1 + below + above) - 1)

    copies = []
    for k, (a, b) in enumerate(OFFSETS):
        rows_src, rows_dst = span(a, rows)
        cols_src, cols_dst = span(b, cols)
        copy = pltpu.make_async_remote_copy(
            src_ref=in_ref.at[rows_src, cols_src],
            dst_ref=out_ref.at[rows_dst, cols_dst],
            send_sem=send_sem.at[k],
            recv_sem=recv_sem.at[k],
            device_id=target(a, b),
            device_id_type=MESH_ID,
        )
        pl.when(has(a))(copy.start)
        copies.append((a, copy))

    own = pltpu.make_async_copy(in_ref, out_ref.at[pl.ds(halo, rows), pl.ds(halo, cols)], own_sem)
    own.start()
    ghost = jnp.zeros((halo,) + out_ref.shape[1:], out_ref.dtype)

    @pl.when(lat == 0)
    def _():
        out_ref[pl.ds(0, halo)] = ghost

    @pl.when(lat == nlat - 1)
    def _():
        out_ref[pl.ds(rows + halo, halo)] = ghost

    for a, copy in copies:
        pl.when(has(a))(copy.wait_send)
        pl.when(has(-a))(copy.wait_recv)
    own.wait()


def halo_exchange(cells, halo):
    rows, cols, chans = cells.shape
    vmem = pl.BlockSpec(memory_space=pltpu.VMEM)
    return pl.pallas_call(
        functools.partial(halo_kernel, halo=halo),
        out_shape=jax.ShapeDtypeStruct((rows + 2 * halo, cols + 2 * halo, chans), cells.dtype),
        in_specs=[vmem],
        out_specs=vmem,
        scratch_shapes=[
            pltpu.SemaphoreType.DMA((8,)),
            pltpu.SemaphoreType.DMA((8,)),
            pltpu.SemaphoreType.DMA(()),
        ],
        compiler_params=pltpu.CompilerParams(collective_id=0, has_side_effects=True),
        interpret=pltpu.InterpretParams(detect_races=True) if INTERPRET else False,
    )(cells)


def exchange(cells, axis, dim, width, closed):
    count = lax.axis_size(axis)
    ends = count if closed else count - 1
    head = lax.slice_in_dim(cells, 0, width, axis=dim)
    tail = lax.slice_in_dim(cells, cells.shape[dim] - width, cells.shape[dim], axis=dim)
    before = lax.ppermute(tail, axis, [(i, (i + 1) % count) for i in range(ends)])
    after = lax.ppermute(head, axis, [((i + 1) % count, i) for i in range(ends)])
    return jnp.concatenate([before, cells, after], axis=dim)


def trim(array, dim, amount):
    return lax.slice_in_dim(array, amount, array.shape[dim] - amount, axis=dim)


def per_device(
    spectrum,
    sea_mask,
    ice_mask,
    depth_class,
    speed_table,
    refraction_table,
    depth_slope,
    wind_speed,
    wind_dir,
    ice_rate,
):
    rows_dev, cols_dev, comps_dev = spectrum.shape
    freqs_dev = comps_dev // NDIR
    halo = 2 * ITERS
    band_index = lax.axis_index("band")
    first_comp = band_index * comps_dev
    local_comp = jnp.arange(comps_dev)
    comp_index = first_comp + local_comp
    spread = (local_comp[None, :] // NDIR == jnp.arange(freqs_dev)[:, None]).astype(jnp.float32)
    heading = 2.0 * math.pi * (comp_index % NDIR).astype(jnp.float32) / NDIR
    face_angle = heading + math.pi / NDIR
    cos_head = jnp.cos(heading)
    sin_head = jnp.sin(heading)
    sin_face = jnp.sin(face_angle)
    cos_face = jnp.cos(face_angle)
    sea_share = sea_mask.astype(jnp.float32)
    ice_share = ice_mask.astype(jnp.float32)
    speed_local = lax.dynamic_slice_in_dim(speed_table, band_index * freqs_dev, freqs_dev, 1)
    refr_local = lax.dynamic_slice_in_dim(refraction_table, band_index * freqs_dev, freqs_dev, 1)
    chosen = (depth_class[..., None] == jnp.arange(speed_table.shape[0]))[..., None]
    group_speed = jnp.sum(jnp.where(chosen, speed_local, 0.0), axis=2) * sea_share[..., None]
    turning = jnp.sum(jnp.where(chosen, refr_local, 0.0), axis=2) * sea_share[..., None]
    turn_x = turning * depth_slope[0][..., None]
    turn_y = turning * depth_slope[1][..., None]
    density = spectrum * sea_share[..., None]

    stacked = jnp.concatenate([density, group_speed, turn_x, turn_y], axis=-1)
    stacked = halo_exchange(stacked, halo)
    density = stacked[..., :comps_dev]
    fields = stacked[..., comps_dev:]

    total_rows = rows_dev * lax.axis_size("lat")
    first_row = lax.axis_index("lat") * rows_dev - halo
    rows_ext = first_row + jnp.arange(rows_dev + 2 * halo)
    inside = ((rows_ext >= 0) & (rows_ext < total_rows))[:, None, None]
    stretch_rows = stretch(rows_ext, total_rows)
    gs_ext = expand(fields[..., :freqs_dev], spread)
    along_x = gs_ext * cos_head * stretch_rows[:, None, None]
    along_y = gs_ext * sin_head
    turns = expand(
        jnp.stack([fields[..., freqs_dev : 2 * freqs_dev], fields[..., 2 * freqs_dev :]]), spread
    )
    along_t = turns[0] * sin_face - turns[1] * cos_face
    for substep in range(ITERS):
        density = advect(density, along_x, 1)
        along_x, along_y, along_t = [trim(a, 1, 2) for a in (along_x, along_y, along_t)]
        density = advect(density, along_y, 0)
        inside = trim(inside, 0, 2)
        density = jnp.where(inside, density, 0.0)
        along_x, along_y, along_t = [trim(a, 0, 2) for a in (along_x, along_y, along_t)]
        density = refract(density, along_t)

    levels = jnp.exp(math.log(freq_ratio) * (comp_index // NDIR).astype(jnp.float32))
    ice_loss = lax.dynamic_slice_in_dim(jnp.repeat(ice_rate, NDIR), first_comp, comps_dev, 0)
    partial = jnp.stack([jnp.sum(density, axis=-1), jnp.sum(density * levels, axis=-1)])
    other = lax.ppermute(partial, "band", [(0, 1), (1, 0)])
    energy_sum = partial[0] + other[0]
    moment = partial[1] + other[1]
    return sources(
        density,
        energy_sum,
        moment,
        levels,
        heading,
        ice_loss,
        sea_share,
        ice_share,
        wind_speed,
        wind_dir,
    )


def solution(mesh):
    return jax.shard_map(
        per_device,
        mesh=mesh,
        in_specs=(
            P("lat", "lon", "band"),
            P("lat", "lon"),
            P("lat", "lon"),
            P("lat", "lon"),
            P(),
            P(),
            P(None, "lat", "lon"),
            P("lat", "lon"),
            P("lat", "lon"),
            P(),
        ),
        out_specs=P("lat", "lon", "band"),
        check_vma=False,
    )
```
